512 devices in a mesh: blk: 32 (over y_hi, z), head: 16 (over y_lo, x, core).
Axes of the slice: x: 4, y: 4 (y_hi: 2, y_lo: 2; y = y_hi * 2 + y_lo), z: 16, core: 2. Of those that a mesh axis runs over, the one named last changes fastest.
Arguments:
- query_rows: bfloat16 [4096, 3072], P(('blk', 'head')), may hold values from -80 to 80, as said below
- key_rows: bfloat16 [4096, 3072], P(('blk', 'head')), may hold values from -5 to 5
- value_rows: bfloat16 [4096, 3072], P(('blk', 'head')), may hold values from -6 to 6
- out_weight: bfloat16 [3072, 3072], P('head'), may hold values from -0.59765625 to 0.59765625
- out_gate: float32 [3072], replicated, may hold values from 0.5 to 2
- radial_mask: int32 [32, 32], replicated, may hold values from 0 to 1, as said below
- span_anchor: int32 [32], replicated, may hold values from 0 to 31, each once
Outputs:
- block_output: bfloat16 [4096, 3072], P(('blk', 'head'))
The draws below stay inside these ranges and needn't reach their ends.
Inputs may be any that keep to these rules, and one draw needn't show every extreme that they name: query_rows is drawn together with key_rows. Entries are 0 or 1 and radial_mask[t][t] = 1 for every tile t. `span_anchor`: each span number appears once.
All inputs are finite; a program needn't handle non-finite values.
Results may differ from the reference program's by a relative error of at most 0.023.
Values may be sent and summed in bfloat16 or wider, within the bound.
A program may use at most 64 MiB of HBM per device.

```python
import math
import jax
import jax.numpy as jnp
from jax import lax

HEADS = 48
HEAD_DIM = 64
D = 3072
TILE = 128
TILES_DEV = 1
SPAN = 128
SEQ = 4096
NT = 32
BAND = 2
N_BLK = 32
N_HEAD = 16


def paired_rows(key):
    base_key = jax.random.fold_in(key, 4242)
    query_key = jax.random.fold_in(base_key, 1)
    keys_key = jax.random.fold_in(base_key, 2)
    scale_key = jax.random.fold_in(base_key, 3)
    queries = jnp.clip(jax.random.normal(query_key, (SEQ, D), jnp.float32), -4.0, 4.0)
    keys_drawn = jnp.clip(jax.random.normal(keys_key, (SEQ, D), jnp.float32), -4.0, 4.0)
    row_scale = jnp.exp(jax.random.uniform(scale_key, (SEQ, 1), jnp.float32, math.log(0.5), math.log(5.0)))
    queries = queries * row_scale
    return (queries, keys_drawn)


def draw_query_rows(key, part):
    return paired_rows(key)[0].astype(jnp.bfloat16)


def draw_key_rows(key, part):
    return paired_rows(key)[1].astype(jnp.bfloat16)


def draw_radial_mask(key, part):
    row_ids = jnp.arange(NT, dtype=jnp.int32)[:, None]
    col_ids = jnp.arange(NT, dtype=jnp.int32)[None, :]
    distance = jnp.abs(row_ids - col_ids)
    drawn = jax.random.randint(jax.random.fold_in(key, 77), (NT, NT), 0, 1 << 20, jnp.int32)
    kept = drawn % jnp.maximum(distance, 1) < BAND
    return jnp.where(distance < BAND, 1, kept.astype(jnp.int32)).astype(jnp.int32)


def levels(key, extent, shards, smallest, top_value):
    factor_of, own = 1.0, jax.random.fold_in(key, 6)
    for axis_at, shards_of in shards:
        draws = jnp.exp(jax.random.uniform(jax.random.fold_in(own, axis_at), (shards_of,), jnp.float32, smallest / len(shards), top_value / len(shards)))
        factor_of = factor_of * jnp.repeat(draws, extent[axis_at] // shards_of).reshape([-1 if axis == axis_at else 1 for axis in range(len(extent))])
    return factor_of


def normal_values(stream_key, dims, width, limit, split=(), kind=jnp.bfloat16):
    values = jax.random.normal(stream_key, dims, jnp.float32) * width
    if len(split) > 0:
        values = levels(stream_key, dims, split, -0.22, 0.18) * values
    return jnp.clip(values, min=-limit, max=limit).astype(kind)


def setup_inputs(seed: int = 0) -> dict:
    splits = jax.random.split(jax.random.key(seed), 8)
    query_rows = draw_query_rows(jax.random.fold_in(splits[7], 71), 0)
    key_rows = draw_key_rows(jax.random.fold_in(splits[7], 71), 0)
    value_rows = normal_values(splits[2], (SEQ, D), 1.0, 6.0, ((0, 512),))
    out_weight = normal_values(splits[3], (D, D), 0.1, 0.59765625, ((0, 16),))
    out_gate = jnp.clip(jnp.exp(jax.random.uniform(splits[4], (D,), jnp.float32, math.log(0.5), math.log(2.0))), 0.5, 2.0)
    radial_mask = draw_radial_mask(jax.random.fold_in(splits[7], 71), 0)
    span_anchor = jax.random.permutation(splits[6], N_BLK).astype(jnp.int32)
    return dict(query_rows=query_rows, key_rows=key_rows, value_rows=value_rows, out_weight=out_weight, out_gate=out_gate, radial_mask=radial_mask, span_anchor=span_anchor)


big_negative = -1.0e30


def reference(query_rows, key_rows, value_rows, out_weight, out_gate, radial_mask, span_anchor):
    scale = HEAD_DIM ** -0.5
    tile_ids = jnp.arange(NT, dtype=jnp.int32)
    anchor = (jnp.repeat(span_anchor, TILES_DEV) * TILES_DEV + tile_ids % TILES_DEV).astype(jnp.int32)
    allowed = radial_mask[anchor][:, anchor] > 0
    allowed_blocks = allowed.reshape(N_BLK, TILES_DEV, NT)
    head_queries = query_rows.reshape(N_BLK, SPAN, HEADS, HEAD_DIM).transpose(2, 0, 1, 3)
    head_keys = key_rows.reshape(SEQ, HEADS, HEAD_DIM).transpose(1, 0, 2)
    head_values = value_rows.reshape(SEQ, HEADS, HEAD_DIM).transpose(1, 0, 2)

    def per_head(inputs):
        queries, keys_one, values_one = inputs

        def per_block(block_inputs):
            block_queries, block_allowed = block_inputs
            scores = jnp.dot(block_queries, keys_one.T, preferred_element_type=jnp.float32) * scale
            visible = jnp.repeat(jnp.repeat(block_allowed, TILE, axis=0), TILE, axis=1)
            masked = jnp.where(visible, scores, big_negative)
            row_max = jnp.max(masked, axis=1, keepdims=True)
            weights = jnp.where(visible, jnp.exp(masked - row_max), 0.0)
            denom = jnp.sum(weights, axis=1, keepdims=True)
            summed = jnp.dot(weights.astype(jnp.bfloat16), values_one, preferred_element_type=jnp.float32)
            return (summed / denom).astype(jnp.bfloat16)

        return lax.map(per_block, (queries, allowed_blocks))

    attended = lax.map(per_head, (head_queries, head_keys, head_values))
    attended = attended.transpose(1, 2, 0, 3).reshape(SEQ, HEADS * HEAD_DIM)
    group_width = (HEADS // N_HEAD) * HEAD_DIM
    group_inputs = attended.reshape(SEQ, N_HEAD, group_width).transpose(1, 0, 2)
    group_weights = out_weight.reshape(N_HEAD, group_width, HEADS * HEAD_DIM)

    def add_group(summed, group_pair):
        group_rows, group_weight = group_pair
        partial_sum = jnp.dot(group_rows, group_weight, preferred_element_type=jnp.float32)
        rounded = lax.optimization_barrier(partial_sum.astype(jnp.bfloat16))
        return summed + rounded.astype(jnp.float32), None

    start_sum = jnp.zeros((SEQ, HEADS * HEAD_DIM), jnp.float32)
    projected, unused = lax.scan(add_group, start_sum, (group_inputs, group_weights))
    return (out_gate[None, :] * projected).astype(jnp.bfloat16)
```

```python
import functools

import jax
import jax.numpy as jnp
from jax import lax
from jax.experimental import pallas as pl
from jax.experimental.pallas import tpu as pltpu
from jax.sharding import PartitionSpec as P

MESH = pl.DeviceIdType.MESH
HEAD_DIM = 64
TILE = 128
HEADS_HERE = 3
WIDTH = HEADS_HERE * HEAD_DIM
LOW = -1e30
UP, DOWN = 0, 1
CHUNK = 512


def kernel(
    groups,
    ring,
    anchor_ref,
    mask_ref,
    q_hbm,
    k_hbm,
    v_hbm,
    w_hbm,
    gate_ref,
    out_ref,
    stage,
    arrived,
    kv,
    queries,
    weights01,
    weights2,
    acc,
    pair_out,
    pair_stat,
    w_vmem,
    partial,
    parts,
    local_sem,
    w_sem,
    a_send,
    a_recv,
    own_sem,
    q_sem,
    ring_send,
    ring_recv,
    pair_send,
    pair_recv,
    p_send,
    p_recv,
    p_own,
):
    f32, bf16 = jnp.float32, jnp.bfloat16
    blk = lax.axis_index("blk")
    me = lax.axis_index("head")
    half = blk // ring
    z = blk % ring
    base = half * ring
    up_blk = base + (z + 1) % ring
    down_blk = base + (z + ring - 1) % ring
    pair_blk = (1 - half) * ring + z
    odd_core = me % 2

    loads = [
        pltpu.make_async_copy(src, stage.at[i], local_sem.at[i])
        for i, src in enumerate((q_hbm, k_hbm, v_hbm))
    ]
    for load in loads:
        load.start()
    w_load = pltpu.make_async_copy(w_hbm, w_vmem, w_sem)
    w_load.start()

    barrier = pltpu.get_barrier_semaphore()

    @pl.loop(1, groups)
    def _(step):
        pl.semaphore_signal(
            barrier, inc=1, device_id=(blk, (me + step) % groups), device_id_type=MESH
        )

    for other in (up_blk, down_blk, pair_blk):
        pl.semaphore_signal(barrier, inc=1, device_id=(other, me), device_id_type=MESH)
    pl.semaphore_wait(barrier, groups - 1 + 3)
    for load in loads:
        load.wait()

    def columns_of(group):
        return pl.ds(pl.multiple_of((group // 2) * (2 * WIDTH) + (group % 2) * 128, 128), 256)

    def exchange(step):
        peer = (me + step) % groups
        return pltpu.make_async_remote_copy(
            src_ref=stage.at[:, :, columns_of(peer)],
            dst_ref=arrived.at[me],
            send_sem=a_send,
            recv_sem=a_recv,
            device_id=(blk, peer),
            device_id_type=MESH,
        )

    @pl.loop(1, groups)
    def _(step):
        exchange(step).start()

    own = pltpu.make_async_copy(stage.at[:, :, columns_of(me)], arrived.at[me], own_sem)
    own.start()
    own.wait()
    all_in = arrived.at[pl.ds(0, groups - 1)]
    pltpu.make_async_copy(all_in, all_in, a_recv).wait()

    lane = lax.broadcasted_iota(jnp.int32, (TILE, 128), 1)
    low_lane = lane < 64
    odd = jnp.full((TILE, 128), odd_core, jnp.int32) == 1

    def gathered(which):
        rows = arrived[:, which].astype(f32).reshape(TILE, 256)
        first, second = rows[:, 0:128], rows[:, 128:256]
        first_r, second_r = pltpu.roll(first, 64, 1), pltpu.roll(second, 64, 1)
        a = jnp.where(odd, jnp.where(low_lane, first_r, second_r), first)
        b = jnp.where(odd, second_r, second)
        return a, b

    def link(direction, kind, step):
        origin = (z + ring - (step - 1)) % ring if direction == UP else (z + step - 1) % ring
        block = kv.at[origin, kind]
        return pltpu.make_async_remote_copy(
            src_ref=block,
            dst_ref=block,
            send_sem=ring_send.at[direction, kind, step],
            recv_sem=ring_recv.at[direction, kind, step],
            device_id=(up_blk if direction == UP else down_blk, me),
            device_id_type=MESH,
        )

    k_a, k_b = gathered(1)
    kv[z, 0, 0:TILE] = k_a.astype(bf16)
    kv[z, 0, TILE:WIDTH] = jnp.where(
        low_lane[0:64], k_b[0:64], pltpu.roll(k_b[64:128], 64, 1)
    ).astype(bf16)
    link(UP, 0, 1).start()
    link(DOWN, 0, 1).start()
    v_a, v_b = gathered(2)
    kv[z, 1, 0:128] = v_a.T.astype(bf16)
    kv[z, 1, 128:WIDTH] = v_b.T[0:64].astype(bf16)
    link(UP, 1, 1).start()
    link(DOWN, 1, 1).start()
    q_a, q_b = gathered(0)
    scale = HEAD_DIM ** (-0.5)
    queries[0, 0:128] = (q_a.T * scale).astype(bf16)
    queries[0, 128:WIDTH] = (q_b.T[0:64] * scale).astype(bf16)
    q_pair = pltpu.make_async_remote_copy(
        src_ref=queries.at[0],
        dst_ref=queries.at[1],
        send_sem=q_sem.at[0],
        recv_sem=q_sem.at[1],
        device_id=(pair_blk, me),
        device_id_type=MESH,
    )
    q_pair.start()
    q_pair.wait_recv()

    weights01[...] = jnp.zeros_like(weights01)
    weights2[...] = jnp.zeros_like(weights2)
    for tile in range(2):
        cols = slice(tile * TILE, tile * TILE + TILE)
        far = slice(2 * TILE + tile * TILE, 3 * TILE + tile * TILE)
        weights01[0:64, cols] = queries[tile, 0:64]
        weights01[64:128, far] = queries[tile, 64:128]
        weights2[0:64, cols] = queries[tile, 128:192]
        weights2[64:128, far] = queries[tile, 128:192]

    acc[...] = jnp.zeros_like(acc)
    anchor_own = anchor_ref[blk]
    anchor_pair = anchor_ref[pair_blk]
    wide_lane = lax.broadcasted_iota(jnp.int32, (1, 2 * TILE), 1)

    def bias_of(origin):
        anchor = anchor_ref[base + origin]
        own_bias = jnp.where(mask_ref[anchor_own, anchor] > 0, f32(0.0), f32(LOW))
        pair_bias = jnp.where(mask_ref[anchor_pair, anchor] > 0, f32(0.0), f32(LOW))
        return jnp.where(
            wide_lane < TILE,
            jnp.full((1, 2 * TILE), own_bias, f32),
            jnp.full((1, 2 * TILE), pair_bias, f32),
        )

    def scores_of(origin):
        bias = bias_of(origin)
        two = jnp.dot(kv[origin, 0, 0:TILE], weights01[...], preferred_element_type=f32)
        one = jnp.dot(kv[origin, 0, TILE:WIDTH], weights2[...], preferred_element_type=f32)
        third = jnp.concatenate([one[:, 0:256], one[:, 256:512]], axis=0)
        return two[:, 0:256] + bias, two[:, 256:512] + bias, third + bias

    def soften(origins, state):
        maxima, sums = state
        scores = [scores_of(origin) for origin in origins]
        new_max, new_sum, probs, scales = [], [], [], []
        for h in range(HEADS_HERE):
            here = [s[h] for s in scores]
            top = maxima[h]
            for s in here:
                top = jnp.maximum(top, jnp.max(s, axis=0, keepdims=True))
            weights = [jnp.exp(s - top) for s in here]
            fade = jnp.exp(maxima[h] - top)
            total = sums[h] * fade
            for w in weights:
                total = total + jnp.sum(w, axis=0, keepdims=True)
            new_max.append(top)
            new_sum.append(total)
            scales.append(fade)
            probs.append([w.astype(bf16) for w in weights])
        return (tuple(new_max), tuple(new_sum)), probs, scales

    def gather_values(origins, probs, scales):
        for h in range(HEADS_HERE):
            rows = slice(h * HEAD_DIM, (h + 1) * HEAD_DIM)
            if len(origins) == 1:
                values, weights = kv[origins[0], 1, rows], probs[h][0]
            else:
                values = jnp.concatenate([kv[o, 1, rows] for o in origins], axis=1)
                weights = jnp.concatenate(probs[h], axis=0)
            acc[h] = acc[h] * scales[h] + jnp.dot(values, weights, preferred_element_type=f32)

    empty_max = jnp.full((1, 2 * TILE), LOW, f32)
    empty_sum = jnp.zeros((1, 2 * TILE), f32)
    state = ((empty_max,) * HEADS_HERE, (empty_sum,) * HEADS_HERE)
    state, probs, scales = soften([z], state)
    gather_values([z], probs, scales)
    far_step = ring // 2

    def ring_step(step, state):
        below, above = (z + ring - step) % ring, (z + step) % ring
        link(UP, 0, step).wait_recv()
        link(UP, 0, step + 1).start()
        link(DOWN, 0, step).wait_recv()

        @pl.when(step < far_step - 1)
        def _():
            link(DOWN, 0, step + 1).start()

        state, probs, scales = soften([below, above], state)
        link(UP, 1, step).wait_recv()

        @pl.when(step < far_step - 1)
        def _():
            link(UP, 1, step + 1).start()

        link(DOWN, 1, step).wait_recv()
        link(DOWN, 1, step + 1).start()
        gather_values([below, above], probs, scales)
        return state

    state = lax.fori_loop(1, far_step, ring_step, state)
    last = (z + far_step) % ring
    link(UP, 0, far_step).wait_recv()
    state, probs, scales = soften([last], state)
    link(DOWN, 1, far_step).wait_recv()
    gather_values([last], probs, scales)
    maxima, sums = state

    own_lanes, pair_lanes = slice(0, TILE), slice(TILE, 2 * TILE)
    for h in range(HEADS_HERE):
        rows = slice(h * HEAD_DIM, (h + 1) * HEAD_DIM)
        inverse = 1.0 / sums[h][:, pair_lanes]
        pair_out[0, rows] = (acc[h, :, pair_lanes] * inverse).astype(bf16)
        pair_stat[0, h : h + 1] = maxima[h][:, pair_lanes]
        pair_stat[0, 4 + h : 5 + h] = sums[h][:, pair_lanes]
    pair_stat[0, 3:4] = jnp.zeros((1, TILE), f32)
    pair_stat[0, 7:8] = jnp.zeros((1, TILE), f32)
    merges = [
        pltpu.make_async_remote_copy(
            src_ref=buffer.at[0],
            dst_ref=buffer.at[1],
            send_sem=pair_send.at[i],
            recv_sem=pair_recv.at[i],
            device_id=(pair_blk, me),
            device_id_type=MESH,
        )
        for i, buffer in enumerate((pair_out, pair_stat))
    ]
    for merge in merges:
        merge.start()
    for merge in merges:
        merge.wait_recv()
    attended = []
    for h in range(HEADS_HERE):
        rows = slice(h * HEAD_DIM, (h + 1) * HEAD_DIM)
        max_a, sum_a = maxima[h][:, own_lanes], sums[h][:, own_lanes]
        max_b, sum_b = pair_stat[1, h : h + 1], pair_stat[1, 4 + h : 5 + h]
        top = jnp.maximum(max_a, max_b)
        fade_a = jnp.exp(max_a - top)
        fade_b = jnp.exp(max_b - top) * sum_b
        inverse = 1.0 / (fade_a * sum_a + fade_b)
        attended.append(
            acc[h, :, own_lanes] * (fade_a * inverse)
            + pair_out[1, rows].astype(f32) * (fade_b * inverse)
        )
    tokens01 = jnp.concatenate(attended[0:2], axis=0).T.astype(bf16)
    tokens2 = jnp.concatenate([attended[2], attended[2]], axis=0).T[:, 0:64].astype(bf16)

    w_load.wait()

    @pl.loop(0, w_vmem.shape[1] // CHUNK)
    def _(c):
        cols = pl.ds(pl.multiple_of(c * CHUNK, CHUNK), CHUNK)
        product = jnp.dot(tokens01, w_vmem[0:128, cols], preferred_element_type=f32)
        product += jnp.dot(tokens2, w_vmem[128:192, cols], preferred_element_type=f32)
        partial[:, :, cols] = product.reshape(groups, TILE // groups, CHUNK).astype(bf16)

    def scatter(step):
        peer = (me + step) % groups
        return pltpu.make_async_remote_copy(
            src_ref=partial.at[peer],
            dst_ref=parts.at[me],
            send_sem=p_send,
            recv_sem=p_recv,
            device_id=(blk, peer),
            device_id_type=MESH,
        )

    @pl.loop(1, groups)
    def _(step):
        scatter(step).start()

    own_part = pltpu.make_async_copy(partial.at[me], parts.at[me], p_own)
    own_part.start()
    own_part.wait()
    all_parts = parts.at[pl.ds(0, groups - 1)]
    pltpu.make_async_copy(all_parts, all_parts, p_recv).wait()

    @pl.loop(0, w_vmem.shape[1] // CHUNK)
    def _(c):
        cols = pl.ds(pl.multiple_of(c * CHUNK, CHUNK), CHUNK)
        summed = jnp.sum(parts[:, :, cols].astype(f32), axis=0)
        out_ref[:, cols] = (summed * gate_ref[:, cols]).astype(bf16)

    pltpu.make_async_copy(all_in, all_in, a_send).wait()
    pltpu.make_async_copy(all_parts, all_parts, p_send).wait()
    q_pair.wait_send()
    for merge in merges:
        merge.wait_send()

    @pl.loop(1, far_step)
    def _(step):
        link(UP, 0, step).wait_send()
        link(UP, 1, step).wait_send()
        link(DOWN, 0, step).wait_send()
        link(DOWN, 1, step).wait_send()

    link(UP, 0, far_step).wait_send()
    link(DOWN, 1, far_step).wait_send()


def body(query_rows, key_rows, value_rows, out_weight, out_gate, radial_mask, span_anchor):
    groups = lax.axis_size("head")
    ring = lax.axis_size("blk") // 2
    rows, width = query_rows.shape
    bf16, f32 = jnp.bfloat16, jnp.float32
    dma, vmem = pltpu.SemaphoreType.DMA, pltpu.VMEM
    in_hbm = pl.BlockSpec(memory_space=pl.ANY)
    in_smem = pl.BlockSpec(memory_space=pltpu.SMEM)
    in_vmem = pl.BlockSpec(memory_space=pltpu.VMEM)
    return pl.pallas_call(
        functools.partial(kernel, groups, ring),
        out_shape=jax.ShapeDtypeStruct((rows, width), bf16),
        in_specs=[in_smem, in_smem, in_hbm, in_hbm, in_hbm, in_hbm, in_vmem],
        out_specs=in_vmem,
        scratch_shapes=[
            vmem((3, rows, width), bf16),
            vmem((groups, 3, rows, 256), bf16),
            vmem((ring, 2, WIDTH, TILE), bf16),
            vmem((2, WIDTH, TILE), bf16),
            vmem((2 * HEAD_DIM, 4 * TILE), bf16),
            vmem((2 * HEAD_DIM, 4 * TILE), bf16),
            vmem((HEADS_HERE, HEAD_DIM, 2 * TILE), f32),
            vmem((2, WIDTH, TILE), bf16),
            vmem((2, 8, TILE), f32),
            vmem((WIDTH, width), bf16),
            vmem((groups, rows, width), bf16),
            vmem((groups, rows, width), bf16),
            dma((3,)),
            dma,
            dma,
            dma,
            dma,
            dma((2,)),
            dma((2, 2, ring // 2 + 1)),
            dma((2, 2, ring // 2 + 1)),
            dma((2,)),
            dma((2,)),
            dma,
            dma,
            dma,
        ],
        compiler_params=pltpu.CompilerParams(
            collective_id=0, has_side_effects=True, vmem_limit_bytes=32 * 1024 * 1024
        ),
        name="radial_attention",
    )(
        span_anchor,
        radial_mask,
        query_rows,
        key_rows,
        value_rows,
        out_weight,
        out_gate.reshape(1, width),
    )


def solution(mesh):
    return jax.shard_map(
        body,
        mesh=mesh,
        in_specs=(
            P(("blk", "head"), None),
            P(("blk", "head"), None),
            P(("blk", "head"), None),
            P("head", None),
            P(),
            P(),
            P(),
        ),
        out_specs=P(("blk", "head"), None),
        check_vma=False,
    )
```

```python
import functools

import jax
import jax.numpy as jnp
from jax import lax
from jax.experimental import pallas as pl
from jax.experimental.pallas import tpu as pltpu
from jax.sharding import PartitionSpec as P

MESH = pl.DeviceIdType.MESH
HEAD_DIM = 64
TILE = 128
HEADS_HERE = 3
WIDTH = HEADS_HERE * HEAD_DIM
LOW = -1e30
UP, DOWN = 0, 1
MEMBERS = 4
QUERIES = MEMBERS * TILE
PIECES = 4
PARTS = 2


def kernel(
    groups,
    span_z,
    anchor_hbm,
    mask_hbm,
    q_hbm,
    k_hbm,
    v_hbm,
    w_hbm,
    gate_hbm,
    out_ref,
    anchor_ref,
    mask_ref,
    gate_ref,
    stage,
    in_kv,
    in_q,
    kv,
    queries,
    weights01,
    weights2,
    acc,
    merge_out,
    merge_in,
    stat_out,
    stat_in,
    w_vmem,
    turned,
    attended,
    partial,
    parts,
    local_sem,
    small_sem,
    w_sem,
    kv_send,
    kv_recv,
    q_send,
    q_recv,
    own_sem,
    share_send,
    share_recv,
    ring_send,
    ring_recv,
    merge_send,
    merge_recv,
    stat_send,
    stat_recv,
    core_sem,
    p_send,
    p_recv,
    p_own,
):
    f32, bf16 = jnp.float32, jnp.bfloat16
    blk = lax.axis_index("blk")
    me = lax.axis_index("head")
    half = blk // span_z
    z = blk % span_z
    parity = z % 2
    ring = span_z // 2
    place = z // 2
    base = half * span_z + parity
    core = me % 2
    chip = me // 2
    chips = groups // 2

    def blk_at(where):
        return base + 2 * where

    up_blk = blk_at((place + 1) % ring)
    down_blk = blk_at((place + ring - 1) % ring)

    def member_blk(r):
        other_half = (half + r // 2) % 2
        other_parity = (parity + r % 2) % 2
        return other_half * span_z + 2 * place + other_parity

    member_blks = [member_blk(r) for r in range(MEMBERS)]
    core_mate = 2 * chip + 1 - core

    loads = [
        pltpu.make_async_copy(src, stage.at[i], local_sem.at[i])
        for i, src in enumerate((k_hbm, v_hbm, q_hbm))
    ]
    for load in loads:
        load.start()
    w_load = pltpu.make_async_copy(w_hbm, w_vmem.at[core], w_sem)
    w_load.start()
    small_loads = [
        pltpu.make_async_copy(src, dst, small_sem.at[i])
        for i, (src, dst) in enumerate(
            ((anchor_hbm, anchor_ref), (mask_hbm, mask_ref), (gate_hbm, gate_ref))
        )
    ]
    for load in small_loads:
        load.start()

    barrier = pltpu.get_barrier_semaphore()

    @pl.loop(1, groups)
    def _(step):
        pl.semaphore_signal(
            barrier, inc=1, device_id=(blk, (me + step) % groups), device_id_type=MESH
        )

    greeted = [up_blk, down_blk] + member_blks[1:]
    for other in greeted:
        pl.semaphore_signal(barrier, inc=1, device_id=(other, me), device_id_type=MESH)
    pl.semaphore_wait(barrier, groups - 1 + len(greeted))
    for load in loads:
        load.wait()

    def columns_of(group):
        return pl.ds(pl.multiple_of((group // 2) * (2 * WIDTH) + (group % 2) * 128, 128), 256)

    slot = core * chips + chip

    def exchange_kv(step):
        peer = (me + step) % groups
        return pltpu.make_async_remote_copy(
            src_ref=stage.at[pl.ds(0, 2), :, columns_of(peer)],
            dst_ref=in_kv.at[slot],
            send_sem=kv_send,
            recv_sem=kv_recv,
            device_id=(blk, peer),
            device_id_type=MESH,
        )

    def exchange_q(step):
        peer = (me + step) % groups
        return pltpu.make_async_remote_copy(
            src_ref=stage.at[2, :, columns_of(peer)],
            dst_ref=in_q.at[slot],
            send_sem=q_send,
            recv_sem=q_recv,
            device_id=(blk, peer),
            device_id_type=MESH,
        )

    @pl.loop(1, groups)
    def _(step):
        exchange_kv(step).start()

    @pl.loop(1, groups)
    def _(step):
        exchange_q(step).start()

    own_kv = pltpu.make_async_copy(
        stage.at[pl.ds(0, 2), :, columns_of(me)], in_kv.at[slot], own_sem.at[0]
    )
    own_q = pltpu.make_async_copy(stage.at[2, :, columns_of(me)], in_q.at[slot], own_sem.at[1])
    own_kv.start()
    own_q.start()
    w_load.wait()
    w_share = pltpu.make_async_remote_copy(
        src_ref=w_vmem.at[core],
        dst_ref=w_vmem.at[core],
        send_sem=share_send,
        recv_sem=share_recv,
        device_id=(blk, core_mate),
        device_id_type=MESH,
    )
    w_share.start()
    own_kv.wait()
    all_kv = in_kv.at[pl.ds(0, groups - 1)]
    all_q = in_q.at[pl.ds(0, groups - 1)]
    pltpu.make_async_copy(all_kv, all_kv, kv_recv).wait()

    lane = lax.broadcasted_iota(jnp.int32, (TILE, 128), 1)
    low_lane = lane < 64
    odd = jnp.full((TILE, 128), core, jnp.int32) == 1

    def aligned(rows):
        rows = rows.astype(f32).reshape(TILE, 256)
        first, second = rows[:, 0:128], rows[:, 128:256]
        first_r, second_r = pltpu.roll(first, 64, 1), pltpu.roll(second, 64, 1)
        a = jnp.where(odd, jnp.where(low_lane, first_r, second_r), first)
        b = jnp.where(odd, second_r, second)
        return a, b

    def link(direction, piece, step):
        where = (place + ring - (step - 1)) % ring if direction == UP else (place + step - 1) % ring
        block = kv.at[where, piece // 2, pl.ds((piece % 2) * (WIDTH // 2), WIDTH // 2)]
        return pltpu.make_async_remote_copy(
            src_ref=block,
            dst_ref=block,
            send_sem=ring_send.at[direction, piece, step],
            recv_sem=ring_recv.at[direction, piece, step],
            device_id=(up_blk if direction == UP else down_blk, me),
            device_id_type=MESH,
        )

    def launch(pieces):
        for piece in pieces:
            link(UP, piece, 1).start()
            link(DOWN, piece, 1).start()

    k_a, k_b = aligned(in_kv[:, 0])
    kv[place, 0, 0:TILE] = k_a.astype(bf16)
    kv[place, 0, TILE:WIDTH] = jnp.where(
        low_lane[0:64], k_b[0:64], pltpu.roll(k_b[64:128], 64, 1)
    ).astype(bf16)
    launch((0, 1))
    v_a, v_b = aligned(in_kv[:, 1])
    kv[place, 1, 0:128] = v_a.T.astype(bf16)
    kv[place, 1, 128:WIDTH] = v_b.T[0:64].astype(bf16)
    launch((2, 3))
    own_q.wait()
    pltpu.make_async_copy(all_q, all_q, q_recv).wait()
    q_a, q_b = aligned(in_q[...])
    scale = HEAD_DIM ** (-0.5)
    queries[0, 0:128] = (q_a.T * scale).astype(bf16)
    queries[0, 128:WIDTH] = (q_b.T[0:64] * scale).astype(bf16)

    def to_member(r, src, dst, send, recv):
        return pltpu.make_async_remote_copy(
            src_ref=src,
            dst_ref=dst,
            send_sem=send,
            recv_sem=recv,
            device_id=(member_blks[r], me),
            device_id_type=MESH,
        )

    others = range(1, MEMBERS)
    q_moves = [
        to_member(r, queries.at[0], queries.at[r], core_sem.at[r], core_sem.at[MEMBERS + r])
        for r in others
    ]
    for move in q_moves:
        move.start()

    weights01[...] = jnp.zeros_like(weights01)
    weights2[...] = jnp.zeros_like(weights2)
    acc[...] = jnp.zeros_like(acc)
    for load in small_loads:
        load.wait()
    anchors = [anchor_ref[member_blks[r]] for r in range(MEMBERS)]
    for move in q_moves:
        move.wait_recv()
    for r in range(MEMBERS):
        cols = slice(r * TILE, (r + 1) * TILE)
        far = slice(QUERIES + r * TILE, QUERIES + (r + 1) * TILE)
        weights01[0:64, cols] = queries[r, 0:64]
        weights01[64:128, far] = queries[r, 64:128]
        weights2[0:64, cols] = queries[r, 128:192]
        weights2[64:128, far] = queries[r, 128:192]

    def bias_of(where):
        anchor = anchor_ref[blk_at(where)]
        return jnp.concatenate(
            [
                jnp.full(
                    (1, TILE), jnp.where(mask_ref[anchors[r], anchor] > 0, f32(0.0), f32(LOW)), f32
                )
                for r in range(MEMBERS)
            ],
            axis=1,
        )

    def scores_of(where):
        bias = bias_of(where)
        two = jnp.dot(kv[where, 0, 0:TILE], weights01[...], preferred_element_type=f32)
        one = jnp.dot(kv[where, 0, TILE:WIDTH], weights2[...], preferred_element_type=f32)
        third = jnp.concatenate([one[:, 0:QUERIES], one[:, QUERIES:]], axis=0)
        return two[:, 0:QUERIES] + bias, two[:, QUERIES:] + bias, third + bias

    def soften(tiles, state):
        maxima, sums = state
        scores = [scores_of(where) for where in tiles]
        new_max, new_sum, probs, scales = [], [], [], []
        for h in range(HEADS_HERE):
            here = [s[h] for s in scores]
            top = maxima[h]
            for s in here:
                top = jnp.maximum(top, jnp.max(s, axis=0, keepdims=True))
            weights = [jnp.exp(s - top) for s in here]
            fade = jnp.exp(maxima[h] - top)
            total = sums[h] * fade
            for w in weights:
                total = total + jnp.sum(w, axis=0, keepdims=True)
            new_max.append(top)
            new_sum.append(total)
            scales.append(fade)
            probs.append([w.astype(bf16) for w in weights])
        return (tuple(new_max), tuple(new_sum)), probs, scales

    def gather_values(tiles, probs, scales):
        for h in range(HEADS_HERE):
            rows = slice(h * HEAD_DIM, (h + 1) * HEAD_DIM)
            if len(tiles) == 1:
                values, weights = kv[tiles[0], 1, rows], probs[h][0]
            else:
                values = jnp.concatenate([kv[t, 1, rows] for t in tiles], axis=1)
                weights = jnp.concatenate(probs[h], axis=0)
            acc[h] = acc[h] * scales[h] + jnp.dot(values, weights, preferred_element_type=f32)

    empty_max = jnp.full((1, QUERIES), LOW, f32)
    empty_sum = jnp.zeros((1, QUERIES), f32)
    state = ((empty_max,) * HEADS_HERE, (empty_sum,) * HEADS_HERE)
    state, probs, scales = soften([place], state)
    gather_values([place], probs, scales)
    far_step = ring // 2

    def ring_step(step, state):
        below, above = (place + ring - step) % ring, (place + step) % ring

        def pass_on(direction, piece, to_far):
            link(direction, piece, step).wait_recv()
            if to_far:
                link(direction, piece, step + 1).start()
            else:

                @pl.when(step < far_step - 1)
                def _():
                    link(direction, piece, step + 1).start()

        for piece in (0, 1):
            pass_on(UP, piece, True)
            pass_on(DOWN, piece, False)
        state, probs, scales = soften([below, above], state)
        for piece in (2, 3):
            pass_on(UP, piece, False)
            pass_on(DOWN, piece, True)
        gather_values([below, above], probs, scales)
        return state

    state = lax.fori_loop(1, far_step, ring_step, state)
    last = (place + far_step) % ring
    for piece in (0, 1):
        link(UP, piece, far_step).wait_recv()
    state, probs, scales = soften([last], state)
    for piece in (2, 3):
        link(DOWN, piece, far_step).wait_recv()
    gather_values([last], probs, scales)
    maxima, sums = state

    stat_out[...] = jnp.zeros_like(stat_out)
    merges = []
    for r in others:
        lanes = slice(r * TILE, (r + 1) * TILE)
        for h in range(HEADS_HERE):
            rows = slice(h * HEAD_DIM, (h + 1) * HEAD_DIM)
            inverse = 1.0 / sums[h][:, lanes]
            merge_out[r, rows] = (acc[h, :, lanes] * inverse).astype(bf16)
            stat_out[r, h : h + 1] = maxima[h][:, lanes]
            stat_out[r, 4 + h : 5 + h] = sums[h][:, lanes]
        merges.append(
            to_member(r, stat_out.at[r], stat_in.at[r], stat_send.at[r], stat_recv.at[r])
        )
        merges.append(
            to_member(r, merge_out.at[r], merge_in.at[r], merge_send.at[r], merge_recv.at[r])
        )
        for merge in merges[-2:]:
            merge.start()
    for merge in merges:
        merge.wait_recv()
    merged = []
    for h in range(HEADS_HERE):
        rows = slice(h * HEAD_DIM, (h + 1) * HEAD_DIM)
        tops = [maxima[h][:, 0:TILE]] + [stat_in[r, h : h + 1] for r in others]
        totals = [sums[h][:, 0:TILE]] + [stat_in[r, 4 + h : 5 + h] for r in others]
        top = functools.reduce(jnp.maximum, tops)
        fades = [jnp.exp(t - top) for t in tops]
        shares = [f * t for f, t in zip(fades, totals)]
        inverse = 1.0 / functools.reduce(jnp.add, shares)
        value = acc[h, :, 0:TILE] * (fades[0] * inverse)
        for r in others:
            value += merge_in[r, rows].astype(f32) * (shares[r] * inverse)
        merged.append(value)
    turned[:, 0:128] = jnp.concatenate(merged[0:2], axis=0).T.astype(bf16)
    turned[:, 128:256] = jnp.concatenate([merged[2], merged[2]], axis=0).T.astype(bf16)
    swap = pltpu.make_async_remote_copy(
        src_ref=turned.at[pl.ds((1 - core) * (TILE // 2), TILE // 2)],
        dst_ref=attended.at[core],
        send_sem=core_sem.at[0],
        recv_sem=core_sem.at[MEMBERS],
        device_id=(blk, core_mate),
        device_id_type=MESH,
    )
    swap.start()
    attended[core] = turned[pl.ds(pl.multiple_of(core * (TILE // 2), TILE // 2), TILE // 2)]
    w_share.wait_recv()
    swap.wait_recv()
    part_width = partial.shape[3]

    def scatter(part, step):
        peer = (chip + step) % chips
        return pltpu.make_async_remote_copy(
            src_ref=partial.at[part, peer],
            dst_ref=parts.at[part, chip],
            send_sem=p_send.at[part],
            recv_sem=p_recv.at[part],
            device_id=(blk, 2 * peer + core),
            device_id_type=MESH,
        )

    own_parts = []
    for part in range(PARTS):
        cols = slice(part * part_width, (part + 1) * part_width)
        product = jnp.zeros((TILE // 2, part_width), f32)
        for c in range(2):
            product += jnp.dot(
                attended[c, :, 0:128], w_vmem[c, 0:128, cols], preferred_element_type=f32
            )
            product += jnp.dot(
                attended[c, :, 128:192], w_vmem[c, 128:192, cols], preferred_element_type=f32
            )
        partial[part] = product.reshape(chips, TILE // groups, part_width).astype(bf16)

        @pl.loop(1, chips)
        def _(step):
            scatter(part, step).start()

        own = pltpu.make_async_copy(
            partial.at[part, chip], parts.at[part, chip], p_own.at[part]
        )
        own.start()
        own_parts.append(own)

    for part in range(PARTS):
        own_parts[part].wait()
        arrived = parts.at[part, pl.ds(0, chips - 1)]
        pltpu.make_async_copy(arrived, arrived, p_recv.at[part]).wait()
        cols = slice(part * part_width, (part + 1) * part_width)
        summed = jnp.sum(parts[part].astype(f32), axis=0)
        out_ref[:, cols] = (summed * gate_ref[:, cols]).astype(bf16)

    pltpu.make_async_copy(all_kv, all_kv, kv_send).wait()
    pltpu.make_async_copy(all_q, all_q, q_send).wait()
    w_share.wait_send()
    swap.wait_send()
    for move in q_moves:
        move.wait_send()
    for merge in merges:
        merge.wait_send()
    for part in range(PARTS):
        sent = parts.at[part, pl.ds(0, chips - 1)]
        pltpu.make_async_copy(sent, sent, p_send.at[part]).wait()

    @pl.loop(1, far_step)
    def _(step):
        for piece in range(PIECES):
            link(UP, piece, step).wait_send()
            link(DOWN, piece, step).wait_send()

    for piece in (0, 1):
        link(UP, piece, far_step).wait_send()
    for piece in (2, 3):
        link(DOWN, piece, far_step).wait_send()


def body(query_rows, key_rows, value_rows, out_weight, out_gate, radial_mask, span_anchor):
    groups = lax.axis_size("head")
    span_z = lax.axis_size("blk") // 2
    ring = span_z // 2
    rows, width = query_rows.shape
    bf16, f32 = jnp.bfloat16, jnp.float32
    dma, vmem = pltpu.SemaphoreType.DMA, pltpu.VMEM
    steps = ring // 2 + 1
    return pl.pallas_call(
        functools.partial(kernel, groups, span_z),
        out_shape=jax.ShapeDtypeStruct((rows, width), bf16),
        in_specs=[pl.BlockSpec(memory_space=pl.ANY)] * 7,
        out_specs=pl.BlockSpec(memory_space=pltpu.VMEM),
        scratch_shapes=[
            pltpu.SMEM(span_anchor.shape, jnp.int32),
            pltpu.SMEM(radial_mask.shape, jnp.int32),
            vmem((1, width), f32),
            vmem((3, rows, width), bf16),
            vmem((groups, 2, rows, 256), bf16),
            vmem((groups, rows, 256), bf16),
            vmem((ring, 2, WIDTH, TILE), bf16),
            vmem((MEMBERS, WIDTH, TILE), bf16),
            vmem((2 * HEAD_DIM, 2 * QUERIES), bf16),
            vmem((2 * HEAD_DIM, 2 * QUERIES), bf16),
            vmem((HEADS_HERE, HEAD_DIM, QUERIES), f32),
            vmem((MEMBERS, WIDTH, TILE), bf16),
            vmem((MEMBERS, WIDTH, TILE), bf16),
            vmem((MEMBERS, 8, TILE), f32),
            vmem((MEMBERS, 8, TILE), f32),
            vmem((2, WIDTH, width), bf16),
            vmem((TILE, 256), bf16),
            vmem((2, TILE // 2, 256), bf16),
            vmem((PARTS, groups // 2, rows, width // PARTS), bf16),
            vmem((PARTS, groups // 2, rows, width // PARTS), bf16),
            dma((3,)),
            dma((3,)),
            dma,
            dma,
            dma,
            dma,
            dma,
            dma((2,)),
            dma,
            dma,
            dma((2, PIECES, steps)),
            dma((2, PIECES, steps)),
            dma((MEMBERS,)),
            dma((MEMBERS,)),
            dma((MEMBERS,)),
            dma((MEMBERS,)),
            dma((2 * MEMBERS,)),
            dma((PARTS,)),
            dma((PARTS,)),
            dma((PARTS,)),
        ],
        compiler_params=pltpu.CompilerParams(
            collective_id=0, has_side_effects=True, vmem_limit_bytes=56 * 1024 * 1024
        ),
        name="radial_attention",
    )(
        span_anchor,
        radial_mask,
        query_rows,
        key_rows,
        value_rows,
        out_weight,
        out_gate.reshape(1, width),
    )


def solution(mesh):
    return jax.shard_map(
        body,
        mesh=mesh,
        in_specs=(
            P(("blk", "head"), None),
            P(("blk", "head"), None),
            P(("blk", "head"), None),
            P("head", None),
            P(),
            P(),
            P(),
        ),
        out_specs=P(("blk", "head"), None),
        check_vma=False,
    )
```

```python
import functools

import jax
import jax.numpy as jnp
from jax import lax
from jax.experimental import pallas as pl
from jax.experimental.pallas import tpu as pltpu
from jax.sharding import PartitionSpec as P

MESH = pl.DeviceIdType.MESH
HEAD_DIM = 64
TILE = 128
HEADS_HERE = 3
WIDTH = HEADS_HERE * HEAD_DIM
LOW = -1e30
UP, DOWN = 0, 1
MEMBERS = 4
QUERIES = MEMBERS * TILE
PIECES = 4
PARTS = 2


def kernel(
    groups,
    span_z,
    anchor_hbm,
    mask_hbm,
    q_hbm,
    k_hbm,
    v_hbm,
    w_hbm,
    gate_hbm,
    out_ref,
    anchor_ref,
    mask_ref,
    gate_ref,
    stage,
    in_kv,
    in_q,
    kv,
    queries,
    weights01,
    weights2,
    acc,
    merge_out,
    merge_in,
    w_vmem,
    turned,
    attended,
    partial,
    parts,
    local_sem,
    small_sem,
    w_sem,
    kv_send,
    kv_recv,
    q_send,
    q_recv,
    own_sem,
    share_send,
    share_recv,
    ring_send,
    ring_recv,
    merge_send,
    merge_recv,
    core_sem,
    p_send,
    p_recv,
    p_own,
):
    f32, bf16 = jnp.float32, jnp.bfloat16
    blk = lax.axis_index("blk")
    me = lax.axis_index("head")
    half = blk // span_z
    z = blk % span_z
    parity = z % 2
    ring = span_z // 2
    place = z // 2
    base = half * span_z + parity
    core = me % 2
    chip = me // 2
    chips = groups // 2

    def blk_at(where):
        return base + 2 * where

    up_blk = blk_at((place + 1) % ring)
    down_blk = blk_at((place + ring - 1) % ring)

    def member_blk(r):
        other_half = (half + r // 2) % 2
        other_parity = (parity + r % 2) % 2
        return other_half * span_z + 2 * place + other_parity

    member_blks = [member_blk(r) for r in range(MEMBERS)]
    core_mate = 2 * chip + 1 - core

    loads = [
        pltpu.make_async_copy(src, stage.at[i], local_sem.at[i])
        for i, src in enumerate((k_hbm, v_hbm, q_hbm))
    ]
    for load in loads:
        load.start()
    w_load = pltpu.make_async_copy(w_hbm, w_vmem.at[core], w_sem)
    w_load.start()
    small_loads = [
        pltpu.make_async_copy(src, dst, small_sem.at[i])
        for i, (src, dst) in enumerate(
            ((anchor_hbm, anchor_ref), (mask_hbm, mask_ref), (gate_hbm, gate_ref))
        )
    ]
    for load in small_loads:
        load.start()

    barrier = pltpu.get_barrier_semaphore()

    @pl.loop(1, groups)
    def _(step):
        pl.semaphore_signal(
            barrier, inc=1, device_id=(blk, (me + step) % groups), device_id_type=MESH
        )

    greeted = [up_blk, down_blk] + member_blks[1:]
    for other in greeted:
        pl.semaphore_signal(barrier, inc=1, device_id=(other, me), device_id_type=MESH)
    pl.semaphore_wait(barrier, groups - 1 + len(greeted))
    for load in loads:
        load.wait()

    def columns_of(group):
        return pl.ds(pl.multiple_of((group // 2) * (2 * WIDTH) + (group % 2) * 128, 128), 256)

    slot = core * chips + chip

    def exchange_kv(step):
        peer = (me + step) % groups
        return pltpu.make_async_remote_copy(
            src_ref=stage.at[pl.ds(0, 2), :, columns_of(peer)],
            dst_ref=in_kv.at[slot],
            send_sem=kv_send,
            recv_sem=kv_recv,
            device_id=(blk, peer),
            device_id_type=MESH,
        )

    def exchange_q(step):
        peer = (me + step) % groups
        return pltpu.make_async_remote_copy(
            src_ref=stage.at[2, :, columns_of(peer)],
            dst_ref=in_q.at[slot],
            send_sem=q_send,
            recv_sem=q_recv,
            device_id=(blk, peer),
            device_id_type=MESH,
        )

    @pl.loop(1, groups)
    def _(step):
        exchange_kv(step).start()

    @pl.loop(1, groups)
    def _(step):
        exchange_q(step).start()

    own_kv = pltpu.make_async_copy(
        stage.at[pl.ds(0, 2), :, columns_of(me)], in_kv.at[slot], own_sem.at[0]
    )
    own_q = pltpu.make_async_copy(stage.at[2, :, columns_of(me)], in_q.at[slot], own_sem.at[1])
    own_kv.start()
    own_q.start()
    w_load.wait()
    w_share = pltpu.make_async_remote_copy(
        src_ref=w_vmem.at[core],
        dst_ref=w_vmem.at[core],
        send_sem=share_send,
        recv_sem=share_recv,
        device_id=(blk, core_mate),
        device_id_type=MESH,
    )
    w_share.start()
    own_kv.wait()
    all_kv = in_kv.at[pl.ds(0, groups - 1)]
    all_q = in_q.at[pl.ds(0, groups - 1)]
    pltpu.make_async_copy(all_kv, all_kv, kv_recv).wait()

    lane = lax.broadcasted_iota(jnp.int32, (TILE, 128), 1)
    low_lane = lane < 64
    odd = jnp.full((TILE, 128), core, jnp.int32) == 1

    def aligned(rows):
        rows = rows.astype(f32).reshape(TILE, 256)
        first, second = rows[:, 0:128], rows[:, 128:256]
        first_r, second_r = pltpu.roll(first, 64, 1), pltpu.roll(second, 64, 1)
        a = jnp.where(odd, jnp.where(low_lane, first_r, second_r), first)
        b = jnp.where(odd, second_r, second)
        return a, b

    def link(direction, piece, step):
        where = (place + ring - (step - 1)) % ring if direction == UP else (place + step - 1) % ring
        block = kv.at[where, piece // 2, pl.ds((piece % 2) * (WIDTH // 2), WIDTH // 2)]
        return pltpu.make_async_remote_copy(
            src_ref=block,
            dst_ref=block,
            send_sem=ring_send.at[direction, piece, step],
            recv_sem=ring_recv.at[direction, piece, step],
            device_id=(up_blk if direction == UP else down_blk, me),
            device_id_type=MESH,
        )

    far_step = ring // 2

    def pass_on(step):
        for piece in range(PIECES):
            for direction in (UP, DOWN):
                link(direction, piece, step).wait_recv()
                if (piece < 2) == (direction == UP):
                    link(direction, piece, step + 1).start()
                else:

                    @pl.when(step < far_step - 1)
                    def _():
                        link(direction, piece, step + 1).start()

    def launch(pieces):
        for piece in pieces:
            link(UP, piece, 1).start()
            link(DOWN, piece, 1).start()

    k_a, k_b = aligned(in_kv[:, 0])
    kv[place, 0, 0:TILE] = k_a.astype(bf16)
    kv[place, 0, TILE:WIDTH] = jnp.where(
        low_lane[0:64], k_b[0:64], pltpu.roll(k_b[64:128], 64, 1)
    ).astype(bf16)
    launch((0, 1))
    v_a, v_b = aligned(in_kv[:, 1])
    kv[place, 1, 0:128] = v_a.T.astype(bf16)
    kv[place, 1, 128:WIDTH] = v_b.T[0:64].astype(bf16)
    launch((2, 3))
    own_q.wait()
    pltpu.make_async_copy(all_q, all_q, q_recv).wait()
    q_a, q_b = aligned(in_q[...])
    scale = HEAD_DIM ** (-0.5)
    queries[0, 0:128] = (q_a.T * scale).astype(bf16)
    queries[0, 128:WIDTH] = (q_b.T[0:64] * scale).astype(bf16)

    def to_member(r, src, dst, send, recv):
        return pltpu.make_async_remote_copy(
            src_ref=src,
            dst_ref=dst,
            send_sem=send,
            recv_sem=recv,
            device_id=(member_blks[r], me),
            device_id_type=MESH,
        )

    others = range(1, MEMBERS)
    q_moves = [
        to_member(r, queries.at[0], queries.at[r], core_sem.at[r], core_sem.at[MEMBERS + r])
        for r in others
    ]
    for move in q_moves:
        move.start()

    weights01[...] = jnp.zeros_like(weights01)
    weights2[...] = jnp.zeros_like(weights2)
    acc[...] = jnp.zeros_like(acc)
    for load in small_loads:
        load.wait()
    anchors = [anchor_ref[member_blks[r]] for r in range(MEMBERS)]
    pass_on(1)
    for move in q_moves:
        move.wait_recv()
    for r in range(MEMBERS):
        cols = slice(r * TILE, (r + 1) * TILE)
        far = slice(QUERIES + r * TILE, QUERIES + (r + 1) * TILE)
        weights01[0:64, cols] = queries[r, 0:64]
        weights01[64:128, far] = queries[r, 64:128]
        weights2[0:64, cols] = queries[r, 128:192]
        weights2[64:128, far] = queries[r, 128:192]

    def bias_of(where):
        anchor = anchor_ref[blk_at(where)]
        return jnp.concatenate(
            [
                jnp.full(
                    (1, TILE), jnp.where(mask_ref[anchors[r], anchor] > 0, f32(0.0), f32(LOW)), f32
                )
                for r in range(MEMBERS)
            ],
            axis=1,
        )

    def scores_of(where):
        bias = bias_of(where)
        two = jnp.dot(kv[where, 0, 0:TILE], weights01[...], preferred_element_type=f32)
        one = jnp.dot(kv[where, 0, TILE:WIDTH], weights2[...], preferred_element_type=f32)
        third = jnp.concatenate([one[:, 0:QUERIES], one[:, QUERIES:]], axis=0)
        return two[:, 0:QUERIES] + bias, two[:, QUERIES:] + bias, third + bias

    def soften(tiles, state):
        maxima, sums = state
        scores = [scores_of(where) for where in tiles]
        new_max, new_sum, probs, scales = [], [], [], []
        for h in range(HEADS_HERE):
            here = [s[h] for s in scores]
            top = maxima[h]
            for s in here:
                top = jnp.maximum(top, jnp.max(s, axis=0, keepdims=True))
            weights = [jnp.exp(s - top) for s in here]
            fade = jnp.exp(maxima[h] - top)
            total = sums[h] * fade
            for w in weights:
                total = total + jnp.sum(w, axis=0, keepdims=True)
            new_max.append(top)
            new_sum.append(total)
            scales.append(fade)
            probs.append([w.astype(bf16) for w in weights])
        return (tuple(new_max), tuple(new_sum)), probs, scales

    def gather_values(tiles, probs, scales):
        for h in range(HEADS_HERE):
            rows = slice(h * HEAD_DIM, (h + 1) * HEAD_DIM)
            if len(tiles) == 1:
                values, weights = kv[tiles[0], 1, rows], probs[h][0]
            else:
                values = jnp.concatenate([kv[t, 1, rows] for t in tiles], axis=1)
                weights = jnp.concatenate(probs[h], axis=0)
            acc[h] = acc[h] * scales[h] + jnp.dot(values, weights, preferred_element_type=f32)

    empty_max = jnp.full((1, QUERIES), LOW, f32)
    empty_sum = jnp.zeros((1, QUERIES), f32)
    state = ((empty_max,) * HEADS_HERE, (empty_sum,) * HEADS_HERE)
    state, probs, scales = soften([place], state)
    gather_values([place], probs, scales)

    def compute_pair(step, state):
        tiles = [(place + ring - step) % ring, (place + step) % ring]
        state, probs, scales = soften(tiles, state)
        gather_values(tiles, probs, scales)
        return state

    def ring_step(step, state):
        pass_on(step)
        return compute_pair(step - 1, state)

    state = lax.fori_loop(2, far_step, ring_step, state)
    state = compute_pair(far_step - 1, state)
    last = (place + far_step) % ring
    for piece in (0, 1):
        link(UP, piece, far_step).wait_recv()
    state, probs, scales = soften([last], state)
    for piece in (2, 3):
        link(DOWN, piece, far_step).wait_recv()
    gather_values([last], probs, scales)
    maxima, sums = state

    levels = [maxima[h] + jnp.log(sums[h]) for h in range(HEADS_HERE)]

    def split_level(level):
        high = level.astype(bf16).astype(f32)
        middle = (level - high).astype(bf16).astype(f32)
        return [high, middle, level - high - middle]

    merges = []
    for r in others:
        lanes = slice(r * TILE, (r + 1) * TILE)
        for h in range(HEADS_HERE):
            rows = slice(h * HEAD_DIM, (h + 1) * HEAD_DIM)
            merge_out[r, rows] = (acc[h, :, lanes] * (1.0 / sums[h][:, lanes])).astype(bf16)
        level_rows = [row for h in range(HEADS_HERE) for row in split_level(levels[h][:, lanes])]
        level_rows.append(jnp.zeros((16 - len(level_rows), TILE), f32))
        merge_out[r, WIDTH : WIDTH + 16] = jnp.concatenate(level_rows, axis=0).astype(bf16)
        merge = to_member(r, merge_out.at[r], merge_in.at[r], merge_send.at[r], merge_recv.at[r])
        merge.start()
        merges.append(merge)
    for merge in merges:
        merge.wait_recv()
    merged = []
    other_levels = [merge_in[r, WIDTH : WIDTH + 16].astype(f32) for r in others]
    for h in range(HEADS_HERE):
        rows = slice(h * HEAD_DIM, (h + 1) * HEAD_DIM)
        tops = [levels[h][:, 0:TILE]] + [
            t[3 * h : 3 * h + 1] + t[3 * h + 1 : 3 * h + 2] + t[3 * h + 2 : 3 * h + 3]
            for t in other_levels
        ]
        top = functools.reduce(jnp.maximum, tops)
        shares = [jnp.exp(t - top) for t in tops]
        inverse = 1.0 / functools.reduce(jnp.add, shares)
        value = acc[h, :, 0:TILE] * (shares[0] * inverse / sums[h][:, 0:TILE])
        for r in others:
            value += merge_in[r, rows].astype(f32) * (shares[r] * inverse)
        merged.append(value)
    turned[:, 0:128] = jnp.concatenate(merged[0:2], axis=0).T.astype(bf16)
    turned[:, 128:256] = jnp.concatenate([merged[2], merged[2]], axis=0).T.astype(bf16)
    swap = pltpu.make_async_remote_copy(
        src_ref=turned.at[pl.ds((1 - core) * (TILE // 2), TILE // 2)],
        dst_ref=attended.at[core],
        send_sem=core_sem.at[0],
        recv_sem=core_sem.at[MEMBERS],
        device_id=(blk, core_mate),
        device_id_type=MESH,
    )
    swap.start()
    attended[core] = turned[pl.ds(pl.multiple_of(core * (TILE // 2), TILE // 2), TILE // 2)]
    w_share.wait_recv()
    swap.wait_recv()
    part_width = partial.shape[3]

    def scatter(part, step):
        peer = (chip + step) % chips
        return pltpu.make_async_remote_copy(
            src_ref=partial.at[part, peer],
            dst_ref=parts.at[part, chip],
            send_sem=p_send.at[part],
            recv_sem=p_recv.at[part],
            device_id=(blk, 2 * peer + core),
            device_id_type=MESH,
        )

    own_parts = []
    for part in range(PARTS):
        cols = slice(part * part_width, (part + 1) * part_width)
        product = jnp.zeros((TILE // 2, part_width), f32)
        for c in range(2):
            product += jnp.dot(
                attended[c, :, 0:128], w_vmem[c, 0:128, cols], preferred_element_type=f32
            )
            product += jnp.dot(
                attended[c, :, 128:192], w_vmem[c, 128:192, cols], preferred_element_type=f32
            )
        partial[part] = product.reshape(chips, TILE // groups, part_width).astype(bf16)

        @pl.loop(1, chips)
        def _(step):
            scatter(part, step).start()

        own = pltpu.make_async_copy(
            partial.at[part, chip], parts.at[part, chip], p_own.at[part]
        )
        own.start()
        own_parts.append(own)

    for part in range(PARTS):
        own_parts[part].wait()
        arrived = parts.at[part, pl.ds(0, chips - 1)]
        pltpu.make_async_copy(arrived, arrived, p_recv.at[part]).wait()
        cols = slice(part * part_width, (part + 1) * part_width)
        summed = jnp.sum(parts[part].astype(f32), axis=0)
        out_ref[:, cols] = (summed * gate_ref[:, cols]).astype(bf16)

    pltpu.make_async_copy(all_kv, all_kv, kv_send).wait()
    pltpu.make_async_copy(all_q, all_q, q_send).wait()
    w_share.wait_send()
    swap.wait_send()
    for move in q_moves:
        move.wait_send()
    for merge in merges:
        merge.wait_send()
    for part in range(PARTS):
        sent = parts.at[part, pl.ds(0, chips - 1)]
        pltpu.make_async_copy(sent, sent, p_send.at[part]).wait()

    @pl.loop(1, far_step)
    def _(step):
        for piece in range(PIECES):
            link(UP, piece, step).wait_send()
            link(DOWN, piece, step).wait_send()

    for piece in (0, 1):
        link(UP, piece, far_step).wait_send()
    for piece in (2, 3):
        link(DOWN, piece, far_step).wait_send()


def body(query_rows, key_rows, value_rows, out_weight, out_gate, radial_mask, span_anchor):
    groups = lax.axis_size("head")
    span_z = lax.axis_size("blk") // 2
    ring = span_z // 2
    rows, width = query_rows.shape
    bf16, f32 = jnp.bfloat16, jnp.float32
    dma, vmem = pltpu.SemaphoreType.DMA, pltpu.VMEM
    steps = ring // 2 + 1
    return pl.pallas_call(
        functools.partial(kernel, groups, span_z),
        out_shape=jax.ShapeDtypeStruct((rows, width), bf16),
        in_specs=[pl.BlockSpec(memory_space=pl.ANY)] * 7,
        out_specs=pl.BlockSpec(memory_space=pltpu.VMEM),
        scratch_shapes=[
            pltpu.SMEM(span_anchor.shape, jnp.int32),
            pltpu.SMEM(radial_mask.shape, jnp.int32),
            vmem((1, width), f32),
            vmem((3, rows, width), bf16),
            vmem((groups, 2, rows, 256), bf16),
            vmem((groups, rows, 256), bf16),
            vmem((ring, 2, WIDTH, TILE), bf16),
            vmem((MEMBERS, WIDTH, TILE), bf16),
            vmem((2 * HEAD_DIM, 2 * QUERIES), bf16),
            vmem((2 * HEAD_DIM, 2 * QUERIES), bf16),
            vmem((HEADS_HERE, HEAD_DIM, QUERIES), f32),
            vmem((MEMBERS, WIDTH + 16, TILE), bf16),
            vmem((MEMBERS, WIDTH + 16, TILE), bf16),
            vmem((2, WIDTH, width), bf16),
            vmem((TILE, 256), bf16),
            vmem((2, TILE // 2, 256), bf16),
            vmem((PARTS, groups // 2, rows, width // PARTS), bf16),
            vmem((PARTS, groups // 2, rows, width // PARTS), bf16),
            dma((3,)),
            dma((3,)),
            dma,
            dma,
            dma,
            dma,
            dma,
            dma((2,)),
            dma,
            dma,
            dma((2, PIECES, steps)),
            dma((2, PIECES, steps)),
            dma((MEMBERS,)),
            dma((MEMBERS,)),
            dma((2 * MEMBERS,)),
            dma((PARTS,)),
            dma((PARTS,)),
            dma((PARTS,)),
        ],
        compiler_params=pltpu.CompilerParams(
            collective_id=0, has_side_effects=True, vmem_limit_bytes=56 * 1024 * 1024
        ),
        name="radial_attention",
    )(
        span_anchor,
        radial_mask,
        query_rows,
        key_rows,
        value_rows,
        out_weight,
        out_gate.reshape(1, width),
    )


def solution(mesh):
    return jax.shard_map(
        body,
        mesh=mesh,
        in_specs=(
            P(("blk", "head"), None),
            P(("blk", "head"), None),
            P(("blk", "head"), None),
            P("head", None),
            P(),
            P(),
            P(),
        ),
        out_specs=P(("blk", "head"), None),
        check_vma=False,
    )
```

```python
import functools

import jax
import jax.numpy as jnp
from jax import lax
from jax.experimental import pallas as pl
from jax.experimental.pallas import tpu as pltpu
from jax.sharding import PartitionSpec as P

MESH = pl.DeviceIdType.MESH
HEAD_DIM = 64
TILE = 128
HEADS_HERE = 3
WIDTH = HEADS_HERE * HEAD_DIM
LOW = -1e30
UP, DOWN = 0, 1
MEMBERS = 4
QUERIES = MEMBERS * TILE
PIECES = 4
PARTS = 4


def kernel(
    groups,
    span_z,
    anchor_hbm,
    mask_hbm,
    q_hbm,
    k_hbm,
    v_hbm,
    w_hbm,
    gate_hbm,
    out_ref,
    anchor_ref,
    mask_ref,
    gate_ref,
    stage,
    raw_q,
    in_kv,
    in_q,
    kv,
    weights01,
    weights2,
    acc,
    merge_out,
    merge_in,
    w_vmem,
    turned,
    attended,
    partial,
    parts,
    local_sem,
    small_sem,
    w_sem,
    kv_send,
    kv_recv,
    q_send,
    q_recv,
    own_sem,
    share_send,
    share_recv,
    ring_send,
    ring_recv,
    merge_send,
    merge_recv,
    core_sem,
    p_send,
    p_recv,
    p_own,
):
    f32, bf16 = jnp.float32, jnp.bfloat16
    blk = lax.axis_index("blk")
    me = lax.axis_index("head")
    half = blk // span_z
    z = blk % span_z
    parity = z % 2
    ring = span_z // 2
    place = z // 2
    base = half * span_z + parity
    core = me % 2
    chip = me // 2
    chips = groups // 2

    def blk_at(where):
        return base + 2 * where

    up_blk = blk_at((place + 1) % ring)
    down_blk = blk_at((place + ring - 1) % ring)

    def member_blk(r):
        other_half = (half + r // 2) % 2
        other_parity = (parity + r % 2) % 2
        return other_half * span_z + 2 * place + other_parity

    member_blks = [member_blk(r) for r in range(MEMBERS)]
    core_mate = 2 * chip + 1 - core

    loads = [
        pltpu.make_async_copy(src, stage.at[i] if i < 2 else raw_q.at[0], local_sem.at[i])
        for i, src in enumerate((k_hbm, v_hbm, q_hbm))
    ]
    for load in loads:
        load.start()
    w_load = pltpu.make_async_copy(w_hbm, w_vmem.at[core], w_sem)
    w_load.start()
    small_loads = [
        pltpu.make_async_copy(src, dst, small_sem.at[i])
        for i, (src, dst) in enumerate(
            ((anchor_hbm, anchor_ref), (mask_hbm, mask_ref), (gate_hbm, gate_ref))
        )
    ]
    for load in small_loads:
        load.start()

    barrier = pltpu.get_barrier_semaphore()

    @pl.loop(1, groups)
    def _(step):
        pl.semaphore_signal(
            barrier, inc=1, device_id=(blk, (me + step) % groups), device_id_type=MESH
        )

    greeted = [up_blk, down_blk] + member_blks[1:]
    for other in greeted:
        pl.semaphore_signal(barrier, inc=1, device_id=(other, me), device_id_type=MESH)
    pl.semaphore_wait(barrier, groups - 1 + len(greeted))
    for load in loads:
        load.wait()

    def columns_of(group):
        return pl.ds(pl.multiple_of((group // 2) * (2 * WIDTH) + (group % 2) * 128, 128), 256)

    slot = core * chips + chip

    def exchange_kv(step):
        peer = (me + step) % groups
        return pltpu.make_async_remote_copy(
            src_ref=stage.at[:, :, columns_of(peer)],
            dst_ref=in_kv.at[slot],
            send_sem=kv_send,
            recv_sem=kv_recv,
            device_id=(blk, peer),
            device_id_type=MESH,
        )

    def exchange_q(step):
        peer = (me + step) % groups
        return pltpu.make_async_remote_copy(
            src_ref=raw_q.at[:, :, columns_of(peer)],
            dst_ref=in_q.at[slot],
            send_sem=q_send,
            recv_sem=q_recv,
            device_id=(blk, peer),
            device_id_type=MESH,
        )

    @pl.loop(1, groups)
    def _(step):
        exchange_kv(step).start()

    def to_member(r, src, dst, send, recv):
        return pltpu.make_async_remote_copy(
            src_ref=src,
            dst_ref=dst,
            send_sem=send,
            recv_sem=recv,
            device_id=(member_blks[r], me),
            device_id_type=MESH,
        )

    others = (3, 1, 2)
    q_moves = [
        to_member(r, raw_q.at[0], raw_q.at[r], core_sem.at[r], core_sem.at[MEMBERS + r])
        for r in others
    ]
    for move in q_moves:
        move.start()

    own_kv = pltpu.make_async_copy(
        stage.at[:, :, columns_of(me)], in_kv.at[slot], own_sem.at[0]
    )
    own_kv.start()
    w_load.wait()
    w_share = pltpu.make_async_remote_copy(
        src_ref=w_vmem.at[core],
        dst_ref=w_vmem.at[core],
        send_sem=share_send,
        recv_sem=share_recv,
        device_id=(blk, core_mate),
        device_id_type=MESH,
    )
    w_share.start()
    own_kv.wait()
    all_kv = in_kv.at[pl.ds(0, groups - 1)]
    all_q = in_q.at[pl.ds(0, groups - 1)]
    pltpu.make_async_copy(all_kv, all_kv, kv_recv).wait()

    lane = lax.broadcasted_iota(jnp.int32, (TILE, 128), 1)
    low_lane = lane < 64
    odd = jnp.full((TILE, 128), core, jnp.int32) == 1

    def aligned(rows):
        rows = rows.astype(f32).reshape(TILE, 256)
        first, second = rows[:, 0:128], rows[:, 128:256]
        first_r, second_r = pltpu.roll(first, 64, 1), pltpu.roll(second, 64, 1)
        a = jnp.where(odd, jnp.where(low_lane, first_r, second_r), first)
        b = jnp.where(odd, second_r, second)
        return a, b

    def link(direction, piece, step):
        where = (place + ring - (step - 1)) % ring if direction == UP else (place + step - 1) % ring
        block = kv.at[where, piece // 2, pl.ds((piece % 2) * (WIDTH // 2), WIDTH // 2)]
        return pltpu.make_async_remote_copy(
            src_ref=block,
            dst_ref=block,
            send_sem=ring_send.at[direction, piece, step],
            recv_sem=ring_recv.at[direction, piece, step],
            device_id=(up_blk if direction == UP else down_blk, me),
            device_id_type=MESH,
        )

    far_step = ring // 2

    def piece_at(direction, turn):
        return turn if direction == UP else (turn + PIECES // 2) % PIECES

    def pass_on(step):
        for turn in range(PIECES):
            for direction in (UP, DOWN):
                piece = piece_at(direction, turn)
                link(direction, piece, step).wait_recv()
                if (piece < 2) == (direction == UP):
                    link(direction, piece, step + 1).start()
                else:

                    @pl.when(step < far_step - 1)
                    def _():
                        link(direction, piece, step + 1).start()

    k_a, k_b = aligned(in_kv[:, 0])
    kv[place, 0, 0:TILE] = k_a.astype(bf16)
    kv[place, 0, TILE:WIDTH] = jnp.where(
        low_lane[0:64], k_b[0:64], pltpu.roll(k_b[64:128], 64, 1)
    ).astype(bf16)
    for piece in (0, 1):
        link(UP, piece, 1).start()
    v_a, v_b = aligned(in_kv[:, 1])
    kv[place, 1, 0:128] = v_a.T.astype(bf16)
    kv[place, 1, 128:WIDTH] = v_b.T[0:64].astype(bf16)
    for piece in (2, 3):
        link(DOWN, piece, 1).start()
    for turn in (2, 3):
        link(UP, piece_at(UP, turn), 1).start()
        link(DOWN, piece_at(DOWN, turn), 1).start()
    for move in q_moves:
        move.wait_recv()

    @pl.loop(1, groups)
    def _(step):
        exchange_q(step).start()

    own_q = pltpu.make_async_copy(raw_q.at[:, :, columns_of(me)], in_q.at[slot], own_sem.at[1])
    own_q.start()
    weights01[...] = jnp.zeros_like(weights01)
    weights2[...] = jnp.zeros_like(weights2)
    acc[...] = jnp.zeros_like(acc)
    for load in small_loads:
        load.wait()
    anchors = [anchor_ref[member_blks[r]] for r in range(MEMBERS)]
    pass_on(1)
    own_q.wait()
    pltpu.make_async_copy(all_q, all_q, q_recv).wait()
    scale = HEAD_DIM ** (-0.5)
    for r in range(MEMBERS):
        q_a, q_b = aligned(in_q[:, r])
        top_q = (q_a.T * scale).astype(bf16)
        last_q = (q_b.T[0:64] * scale).astype(bf16)
        cols = slice(r * TILE, (r + 1) * TILE)
        far = slice(QUERIES + r * TILE, QUERIES + (r + 1) * TILE)
        weights01[0:64, cols] = top_q[0:64]
        weights01[64:128, far] = top_q[64:128]
        weights2[0:64, cols] = last_q
        weights2[64:128, far] = last_q

    def bias_of(where):
        anchor = anchor_ref[blk_at(where)]
        return jnp.concatenate(
            [
                jnp.full(
                    (1, TILE), jnp.where(mask_ref[anchors[r], anchor] > 0, f32(0.0), f32(LOW)), f32
                )
                for r in range(MEMBERS)
            ],
            axis=1,
        )

    def scores_of(where):
        bias = bias_of(where)
        two = jnp.dot(kv[where, 0, 0:TILE], weights01[...], preferred_element_type=f32)
        one = jnp.dot(kv[where, 0, TILE:WIDTH], weights2[...], preferred_element_type=f32)
        third = jnp.concatenate([one[:, 0:QUERIES], one[:, QUERIES:]], axis=0)
        return two[:, 0:QUERIES] + bias, two[:, QUERIES:] + bias, third + bias

    def soften(tiles, state):
        maxima, sums = state
        scores = [scores_of(where) for where in tiles]
        new_max, new_sum, probs, scales = [], [], [], []
        for h in range(HEADS_HERE):
            here = [s[h] for s in scores]
            top = maxima[h]
            for s in here:
                top = jnp.maximum(top, jnp.max(s, axis=0, keepdims=True))
            weights = [jnp.exp(s - top) for s in here]
            fade = jnp.exp(maxima[h] - top)
            total = sums[h] * fade
            for w in weights:
                total = total + jnp.sum(w, axis=0, keepdims=True)
            new_max.append(top)
            new_sum.append(total)
            scales.append(fade)
            probs.append([w.astype(bf16) for w in weights])
        return (tuple(new_max), tuple(new_sum)), probs, scales

    def gather_values(tiles, probs, scales):
        for h in range(HEADS_HERE):
            rows = slice(h * HEAD_DIM, (h + 1) * HEAD_DIM)
            if len(tiles) == 1:
                values, weights = kv[tiles[0], 1, rows], probs[h][0]
            else:
                values = jnp.concatenate([kv[t, 1, rows] for t in tiles], axis=1)
                weights = jnp.concatenate(probs[h], axis=0)
            acc[h] = acc[h] * scales[h] + jnp.dot(values, weights, preferred_element_type=f32)

    empty_max = jnp.full((1, QUERIES), LOW, f32)
    empty_sum = jnp.zeros((1, QUERIES), f32)
    state = ((empty_max,) * HEADS_HERE, (empty_sum,) * HEADS_HERE)
    state, probs, scales = soften([place], state)
    gather_values([place], probs, scales)

    def compute_pair(step, state):
        tiles = [(place + ring - step) % ring, (place + step) % ring]
        state, probs, scales = soften(tiles, state)
        gather_values(tiles, probs, scales)
        return state

    def ring_step(step, state):
        pass_on(step)
        return compute_pair(step - 1, state)

    state = lax.fori_loop(2, far_step, ring_step, state)
    state = compute_pair(far_step - 1, state)
    last = (place + far_step) % ring
    for piece in (0, 1):
        link(UP, piece, far_step).wait_recv()
    state, probs, scales = soften([last], state)
    for piece in (2, 3):
        link(DOWN, piece, far_step).wait_recv()
    gather_values([last], probs, scales)
    maxima, sums = state

    levels = [maxima[h] + jnp.log(sums[h]) for h in range(HEADS_HERE)]

    def split_level(level):
        high = level.astype(bf16).astype(f32)
        middle = (level - high).astype(bf16).astype(f32)
        return [high, middle, level - high - middle]

    merges = []
    for r in others:
        lanes = slice(r * TILE, (r + 1) * TILE)
        for h in range(HEADS_HERE):
            rows = slice(h * HEAD_DIM, (h + 1) * HEAD_DIM)
            merge_out[r, rows] = (acc[h, :, lanes] * (1.0 / sums[h][:, lanes])).astype(bf16)
        level_rows = [row for h in range(HEADS_HERE) for row in split_level(levels[h][:, lanes])]
        level_rows.append(jnp.zeros((16 - len(level_rows), TILE), f32))
        merge_out[r, WIDTH : WIDTH + 16] = jnp.concatenate(level_rows, axis=0).astype(bf16)
        merge = to_member(r, merge_out.at[r], merge_in.at[r], merge_send.at[r], merge_recv.at[r])
        merge.start()
        merges.append(merge)
    for merge in merges:
        merge.wait_recv()
    merged = []
    ranks = range(1, MEMBERS)
    other_levels = [merge_in[r, WIDTH : WIDTH + 16].astype(f32) for r in ranks]
    for h in range(HEADS_HERE):
        rows = slice(h * HEAD_DIM, (h + 1) * HEAD_DIM)
        tops = [levels[h][:, 0:TILE]] + [
            t[3 * h : 3 * h + 1] + t[3 * h + 1 : 3 * h + 2] + t[3 * h + 2 : 3 * h + 3]
            for t in other_levels
        ]
        top = functools.reduce(jnp.maximum, tops)
        shares = [jnp.exp(t - top) for t in tops]
        inverse = 1.0 / functools.reduce(jnp.add, shares)
        value = acc[h, :, 0:TILE] * (shares[0] * inverse / sums[h][:, 0:TILE])
        for r in ranks:
            value += merge_in[r, rows].astype(f32) * (shares[r] * inverse)
        merged.append(value)
    turned[:, 0:128] = jnp.concatenate(merged[0:2], axis=0).T.astype(bf16)
    turned[:, 128:256] = jnp.concatenate([merged[2], merged[2]], axis=0).T.astype(bf16)
    swap = pltpu.make_async_remote_copy(
        src_ref=turned.at[pl.ds((1 - core) * (TILE // 2), TILE // 2)],
        dst_ref=attended.at[core],
        send_sem=core_sem.at[0],
        recv_sem=core_sem.at[MEMBERS],
        device_id=(blk, core_mate),
        device_id_type=MESH,
    )
    swap.start()
    attended[core] = turned[pl.ds(pl.multiple_of(core * (TILE // 2), TILE // 2), TILE // 2)]
    w_share.wait_recv()
    swap.wait_recv()
    part_width = partial.shape[3]

    def scatter(part, step):
        peer = (chip + step) % chips
        return pltpu.make_async_remote_copy(
            src_ref=partial.at[part, peer],
            dst_ref=parts.at[part, chip],
            send_sem=p_send.at[part],
            recv_sem=p_recv.at[part],
            device_id=(blk, 2 * peer + core),
            device_id_type=MESH,
        )

    own_parts = []
    for part in range(PARTS):
        cols = slice(part * part_width, (part + 1) * part_width)
        product = jnp.zeros((TILE // 2, part_width), f32)
        for c in range(2):
            product += jnp.dot(
                attended[c, :, 0:128], w_vmem[c, 0:128, cols], preferred_element_type=f32
            )
            product += jnp.dot(
                attended[c, :, 128:192], w_vmem[c, 128:192, cols], preferred_element_type=f32
            )
        partial[part] = product.reshape(chips, TILE // groups, part_width).astype(bf16)

        @pl.loop(1, chips)
        def _(step):
            scatter(part, step).start()

        own = pltpu.make_async_copy(
            partial.at[part, chip], parts.at[part, chip], p_own.at[part]
        )
        own.start()
        own_parts.append(own)

    for part in range(PARTS):
        own_parts[part].wait()
        arrived = parts.at[part, pl.ds(0, chips - 1)]
        pltpu.make_async_copy(arrived, arrived, p_recv.at[part]).wait()
        cols = slice(part * part_width, (part + 1) * part_width)
        summed = jnp.sum(parts[part].astype(f32), axis=0)
        out_ref[:, cols] = (summed * gate_ref[:, cols]).astype(bf16)

    pltpu.make_async_copy(all_kv, all_kv, kv_send).wait()
    pltpu.make_async_copy(all_q, all_q, q_send).wait()
    w_share.wait_send()
    swap.wait_send()
    for move in q_moves:
        move.wait_send()
    for merge in merges:
        merge.wait_send()
    for part in range(PARTS):
        sent = parts.at[part, pl.ds(0, chips - 1)]
        pltpu.make_async_copy(sent, sent, p_send.at[part]).wait()

    @pl.loop(1, far_step)
    def _(step):
        for piece in range(PIECES):
            link(UP, piece, step).wait_send()
            link(DOWN, piece, step).wait_send()

    for piece in (0, 1):
        link(UP, piece, far_step).wait_send()
    for piece in (2, 3):
        link(DOWN, piece, far_step).wait_send()


def body(query_rows, key_rows, value_rows, out_weight, out_gate, radial_mask, span_anchor):
    groups = lax.axis_size("head")
    span_z = lax.axis_size("blk") // 2
    ring = span_z // 2
    rows, width = query_rows.shape
    bf16, f32 = jnp.bfloat16, jnp.float32
    dma, vmem = pltpu.SemaphoreType.DMA, pltpu.VMEM
    steps = ring // 2 + 1
    return pl.pallas_call(
        functools.partial(kernel, groups, span_z),
        out_shape=jax.ShapeDtypeStruct((rows, width), bf16),
        in_specs=[pl.BlockSpec(memory_space=pl.ANY)] * 7,
        out_specs=pl.BlockSpec(memory_space=pltpu.VMEM),
        scratch_shapes=[
            pltpu.SMEM(span_anchor.shape, jnp.int32),
            pltpu.SMEM(radial_mask.shape, jnp.int32),
            vmem((1, width), f32),
            vmem((2, rows, width), bf16),
            vmem((MEMBERS, rows, width), bf16),
            vmem((groups, 2, rows, 256), bf16),
            vmem((groups, MEMBERS, rows, 256), bf16),
            vmem((ring, 2, WIDTH, TILE), bf16),
            vmem((2 * HEAD_DIM, 2 * QUERIES), bf16),
            vmem((2 * HEAD_DIM, 2 * QUERIES), bf16),
            vmem((HEADS_HERE, HEAD_DIM, QUERIES), f32),
            vmem((MEMBERS, WIDTH + 16, TILE), bf16),
            vmem((MEMBERS, WIDTH + 16, TILE), bf16),
            vmem((2, WIDTH, width), bf16),
            vmem((TILE, 256), bf16),
            vmem((2, TILE // 2, 256), bf16),
            vmem((PARTS, groups // 2, rows, width // PARTS), bf16),
            vmem((PARTS, groups // 2, rows, width // PARTS), bf16),
            dma((3,)),
            dma((3,)),
            dma,
            dma,
            dma,
            dma,
            dma,
            dma((2,)),
            dma,
            dma,
            dma((2, PIECES, steps)),
            dma((2, PIECES, steps)),
            dma((MEMBERS,)),
            dma((MEMBERS,)),
            dma((2 * MEMBERS,)),
            dma((PARTS,)),
            dma((PARTS,)),
            dma((PARTS,)),
        ],
        compiler_params=pltpu.CompilerParams(
            collective_id=0, has_side_effects=True, vmem_limit_bytes=56 * 1024 * 1024
        ),
        name="radial_attention",
    )(
        span_anchor,
        radial_mask,
        query_rows,
        key_rows,
        value_rows,
        out_weight,
        out_gate.reshape(1, width),
    )


def solution(mesh):
    return jax.shard_map(
        body,
        mesh=mesh,
        in_specs=(
            P(("blk", "head"), None),
            P(("blk", "head"), None),
            P(("blk", "head"), None),
            P("head", None),
            P(),
            P(),
            P(),
        ),
        out_specs=P(("blk", "head"), None),
        check_vma=False,
    )
```

```python
import functools

import jax
import jax.numpy as jnp
from jax import lax
from jax.experimental import pallas as pl
from jax.experimental.pallas import tpu as pltpu
from jax.sharding import PartitionSpec as P

MESH = pl.DeviceIdType.MESH
HEAD_DIM = 64
TILE = 128
HEADS_HERE = 3
WIDTH = HEADS_HERE * HEAD_DIM
LOW = -1e30
UP, DOWN = 0, 1
MEMBERS = 4
QUERIES = MEMBERS * TILE
PIECES = 4
PARTS = 4


def kernel(
    groups,
    span_z,
    anchor_hbm,
    mask_hbm,
    q_hbm,
    k_hbm,
    v_hbm,
    w_hbm,
    gate_hbm,
    out_ref,
    anchor_ref,
    mask_ref,
    gate_ref,
    stage,
    raw_q,
    in_kv,
    in_q,
    kv,
    weights01,
    weights2,
    acc,
    merge_out,
    merge_in,
    w_vmem,
    partial,
    parts,
    local_sem,
    small_sem,
    w_sem,
    kv_send,
    kv_recv,
    q_send,
    q_recv,
    own_sem,
    share_send,
    share_recv,
    ring_send,
    ring_recv,
    merge_send,
    merge_recv,
    core_sem,
    p_send,
    p_recv,
    p_own,
):
    f32, bf16 = jnp.float32, jnp.bfloat16
    blk = lax.axis_index("blk")
    me = lax.axis_index("head")
    half = blk // span_z
    z = blk % span_z
    parity = z % 2
    ring = span_z // 2
    place = z // 2
    base = half * span_z + parity
    core = me % 2
    chip = me // 2
    chips = groups // 2

    def blk_at(where):
        return base + 2 * where

    up_blk = blk_at((place + 1) % ring)
    down_blk = blk_at((place + ring - 1) % ring)

    def member_blk(r):
        other_half = (half + r // 2) % 2
        other_parity = (parity + r % 2) % 2
        return other_half * span_z + 2 * place + other_parity

    member_blks = [member_blk(r) for r in range(MEMBERS)]
    core_mate = 2 * chip + 1 - core

    loads = [
        pltpu.make_async_copy(src, stage.at[i] if i < 2 else raw_q.at[0], local_sem.at[i])
        for i, src in enumerate((k_hbm, v_hbm, q_hbm))
    ]
    for load in loads:
        load.start()
    w_load = pltpu.make_async_copy(w_hbm, w_vmem.at[core], w_sem)
    w_load.start()
    small_loads = [
        pltpu.make_async_copy(src, dst, small_sem.at[i])
        for i, (src, dst) in enumerate(
            ((anchor_hbm, anchor_ref), (mask_hbm, mask_ref), (gate_hbm, gate_ref))
        )
    ]
    for load in small_loads:
        load.start()

    barrier = pltpu.get_barrier_semaphore()

    @pl.loop(1, groups)
    def _(step):
        pl.semaphore_signal(
            barrier, inc=1, device_id=(blk, (me + step) % groups), device_id_type=MESH
        )

    greeted = [up_blk, down_blk] + member_blks[1:]
    for other in greeted:
        pl.semaphore_signal(barrier, inc=1, device_id=(other, me), device_id_type=MESH)
    for other in member_blks[1:]:
        pl.semaphore_signal(barrier, inc=1, device_id=(other, core_mate), device_id_type=MESH)
    pl.semaphore_wait(barrier, groups - 1 + len(greeted) + MEMBERS - 1)
    for load in loads:
        load.wait()

    def columns_of(group):
        return pl.ds(pl.multiple_of((group // 2) * (2 * WIDTH) + (group % 2) * 128, 128), 256)

    slot = core * chips + chip

    def exchange_kv(step):
        peer = (me + step) % groups
        return pltpu.make_async_remote_copy(
            src_ref=stage.at[:, :, columns_of(peer)],
            dst_ref=in_kv.at[slot],
            send_sem=kv_send,
            recv_sem=kv_recv,
            device_id=(blk, peer),
            device_id_type=MESH,
        )

    def exchange_q(step):
        peer = (me + step) % groups
        return pltpu.make_async_remote_copy(
            src_ref=raw_q.at[:, :, columns_of(peer)],
            dst_ref=in_q.at[slot],
            send_sem=q_send,
            recv_sem=q_recv,
            device_id=(blk, peer),
            device_id_type=MESH,
        )

    @pl.loop(1, groups)
    def _(step):
        exchange_kv(step).start()

    def to_member(r, src, dst, send, recv):
        return pltpu.make_async_remote_copy(
            src_ref=src,
            dst_ref=dst,
            send_sem=send,
            recv_sem=recv,
            device_id=(member_blks[r], me),
            device_id_type=MESH,
        )

    others = (3, 1, 2)
    q_moves = [
        to_member(r, raw_q.at[0], raw_q.at[r], core_sem.at[r], core_sem.at[MEMBERS + r])
        for r in others
    ]
    for move in q_moves:
        move.start()

    own_kv = pltpu.make_async_copy(
        stage.at[:, :, columns_of(me)], in_kv.at[slot], own_sem.at[0]
    )
    own_kv.start()
    w_load.wait()
    w_share = pltpu.make_async_remote_copy(
        src_ref=w_vmem.at[core],
        dst_ref=w_vmem.at[core],
        send_sem=share_send,
        recv_sem=share_recv,
        device_id=(blk, core_mate),
        device_id_type=MESH,
    )
    w_share.start()
    own_kv.wait()
    all_kv = in_kv.at[pl.ds(0, groups - 1)]
    all_q = in_q.at[pl.ds(0, groups - 1)]
    pltpu.make_async_copy(all_kv, all_kv, kv_recv).wait()

    lane = lax.broadcasted_iota(jnp.int32, (TILE, 128), 1)
    low_lane = lane < 64
    odd = jnp.full((TILE, 128), core, jnp.int32) == 1

    def aligned(rows):
        rows = rows.astype(f32).reshape(TILE, 256)
        first, second = rows[:, 0:128], rows[:, 128:256]
        first_r, second_r = pltpu.roll(first, 64, 1), pltpu.roll(second, 64, 1)
        a = jnp.where(odd, jnp.where(low_lane, first_r, second_r), first)
        b = jnp.where(odd, second_r, second)
        return a, b

    def link(direction, piece, step):
        where = (place + ring - (step - 1)) % ring if direction == UP else (place + step - 1) % ring
        block = kv.at[where, piece // 2, pl.ds((piece % 2) * (WIDTH // 2), WIDTH // 2)]
        return pltpu.make_async_remote_copy(
            src_ref=block,
            dst_ref=block,
            send_sem=ring_send.at[direction, piece, step],
            recv_sem=ring_recv.at[direction, piece, step],
            device_id=(up_blk if direction == UP else down_blk, me),
            device_id_type=MESH,
        )

    far_step = ring // 2

    def piece_at(direction, turn):
        return turn if direction == UP else (turn + PIECES // 2) % PIECES

    def pass_on(step):
        for turn in range(PIECES):
            for direction in (UP, DOWN):
                piece = piece_at(direction, turn)
                link(direction, piece, step).wait_recv()
                if (piece < 2) == (direction == UP):
                    link(direction, piece, step + 1).start()
                else:

                    @pl.when(step < far_step - 1)
                    def _():
                        link(direction, piece, step + 1).start()

    k_a, k_b = aligned(in_kv[:, 0])
    kv[place, 0, 0:TILE] = k_a.astype(bf16)
    kv[place, 0, TILE:WIDTH] = jnp.where(
        low_lane[0:64], k_b[0:64], pltpu.roll(k_b[64:128], 64, 1)
    ).astype(bf16)
    for piece in (0, 1):
        link(UP, piece, 1).start()
    v_a, v_b = aligned(in_kv[:, 1])
    kv[place, 1, 0:128] = v_a.T.astype(bf16)
    kv[place, 1, 128:WIDTH] = v_b.T[0:64].astype(bf16)
    for piece in (2, 3):
        link(DOWN, piece, 1).start()
    for turn in (2, 3):
        link(UP, piece_at(UP, turn), 1).start()
        link(DOWN, piece_at(DOWN, turn), 1).start()
    for move in q_moves:
        move.wait_recv()

    @pl.loop(1, groups)
    def _(step):
        exchange_q(step).start()

    own_q = pltpu.make_async_copy(raw_q.at[:, :, columns_of(me)], in_q.at[slot], own_sem.at[1])
    own_q.start()
    weights01[...] = jnp.zeros_like(weights01)
    weights2[...] = jnp.zeros_like(weights2)
    acc[...] = jnp.zeros_like(acc)
    for load in small_loads:
        load.wait()
    anchors = [anchor_ref[member_blks[r]] for r in range(MEMBERS)]
    pass_on(1)
    own_q.wait()
    pltpu.make_async_copy(all_q, all_q, q_recv).wait()
    scale = HEAD_DIM ** (-0.5)
    for r in range(MEMBERS):
        q_a, q_b = aligned(in_q[:, r])
        top_q = (q_a.T * scale).astype(bf16)
        last_q = (q_b.T[0:64] * scale).astype(bf16)
        cols = slice(r * TILE, (r + 1) * TILE)
        far = slice(QUERIES + r * TILE, QUERIES + (r + 1) * TILE)
        weights01[0:64, cols] = top_q[0:64]
        weights01[64:128, far] = top_q[64:128]
        weights2[0:64, cols] = last_q
        weights2[64:128, far] = last_q

    def bias_of(where):
        anchor = anchor_ref[blk_at(where)]
        return jnp.concatenate(
            [
                jnp.full(
                    (1, TILE), jnp.where(mask_ref[anchors[r], anchor] > 0, f32(0.0), f32(LOW)), f32
                )
                for r in range(MEMBERS)
            ],
            axis=1,
        )

    def scores_of(where):
        bias = bias_of(where)
        two = jnp.dot(kv[where, 0, 0:TILE], weights01[...], preferred_element_type=f32)
        one = jnp.dot(kv[where, 0, TILE:WIDTH], weights2[...], preferred_element_type=f32)
        third = jnp.concatenate([one[:, 0:QUERIES], one[:, QUERIES:]], axis=0)
        return two[:, 0:QUERIES] + bias, two[:, QUERIES:] + bias, third + bias

    def soften(tiles, state):
        maxima, sums = state
        scores = [scores_of(where) for where in tiles]
        new_max, new_sum, probs, scales = [], [], [], []
        for h in range(HEADS_HERE):
            here = [s[h] for s in scores]
            top = maxima[h]
            for s in here:
                top = jnp.maximum(top, jnp.max(s, axis=0, keepdims=True))
            weights = [jnp.exp(s - top) for s in here]
            fade = jnp.exp(maxima[h] - top)
            total = sums[h] * fade
            for w in weights:
                total = total + jnp.sum(w, axis=0, keepdims=True)
            new_max.append(top)
            new_sum.append(total)
            scales.append(fade)
            probs.append([w.astype(bf16) for w in weights])
        return (tuple(new_max), tuple(new_sum)), probs, scales

    def gather_values(tiles, probs, scales):
        for h in range(HEADS_HERE):
            rows = slice(h * HEAD_DIM, (h + 1) * HEAD_DIM)
            if len(tiles) == 1:
                values, weights = kv[tiles[0], 1, rows], probs[h][0]
            else:
                values = jnp.concatenate([kv[t, 1, rows] for t in tiles], axis=1)
                weights = jnp.concatenate(probs[h], axis=0)
            acc[h] = acc[h] * scales[h] + jnp.dot(values, weights, preferred_element_type=f32)

    empty_max = jnp.full((1, QUERIES), LOW, f32)
    empty_sum = jnp.zeros((1, QUERIES), f32)
    state = ((empty_max,) * HEADS_HERE, (empty_sum,) * HEADS_HERE)
    state, probs, scales = soften([place], state)
    gather_values([place], probs, scales)

    def compute_pair(step, state):
        tiles = [(place + ring - step) % ring, (place + step) % ring]
        state, probs, scales = soften(tiles, state)
        gather_values(tiles, probs, scales)
        return state

    def ring_step(step, state):
        pass_on(step)
        return compute_pair(step - 1, state)

    state = lax.fori_loop(2, far_step, ring_step, state)
    state = compute_pair(far_step - 1, state)
    last = (place + far_step) % ring
    for piece in (0, 1):
        link(UP, piece, far_step).wait_recv()
    state, probs, scales = soften([last], state)
    for piece in (2, 3):
        link(DOWN, piece, far_step).wait_recv()
    gather_values([last], probs, scales)
    maxima, sums = state

    def split_level(level):
        high = level.astype(bf16).astype(f32)
        middle = (level - high).astype(bf16).astype(f32)
        return [high, middle, level - high - middle]

    levels = [row for h in range(HEADS_HERE) for row in split_level(maxima[h] + jnp.log(sums[h]))]
    levels = jnp.concatenate(levels + [jnp.zeros((16 - len(levels), QUERIES), f32)], axis=0)
    folded = WIDTH // 2
    low16, low_f = low_lane[0:16], low_lane[0:folded]

    def fold(r):
        lanes = slice(r * TILE, (r + 1) * TILE)
        value = jnp.concatenate(
            [acc[h, :, lanes] * (1.0 / sums[h][:, lanes]) for h in range(HEADS_HERE)], axis=0
        )
        upper, lower = value[0:folded], value[folded:WIDTH]
        level = levels[:, lanes]
        level_r = pltpu.roll(level, 64, 1)
        merge_out[r, 0, 0:folded] = jnp.where(low_f, upper, pltpu.roll(lower, 64, 1)).astype(bf16)
        merge_out[r, 1, 0:folded] = jnp.where(low_f, pltpu.roll(upper, 64, 1), lower).astype(bf16)
        merge_out[r, 0, folded:] = jnp.where(low16, level, level_r).astype(bf16)
        merge_out[r, 1, folded:] = jnp.where(low16, level_r, level).astype(bf16)

    merges = []
    for r in others:
        fold(r)
        for c in range(2):
            merge = pltpu.make_async_remote_copy(
                src_ref=merge_out.at[r, c],
                dst_ref=merge_in.at[core, r],
                send_sem=merge_send.at[r, c],
                recv_sem=merge_recv.at[r, core],
                device_id=(member_blks[r], 2 * chip + c),
                device_id_type=MESH,
            )
            merge.start()
            merges.append(merge)
    fold(0)
    swap = pltpu.make_async_remote_copy(
        src_ref=merge_out.at[0, 1 - core],
        dst_ref=merge_in.at[core, 0],
        send_sem=merge_send.at[0, 0],
        recv_sem=merge_recv.at[0, core],
        device_id=(blk, core_mate),
        device_id_type=MESH,
    )
    swap.start()
    merge_in[core, 0] = merge_out[0, core]
    w_share.wait_recv()
    pltpu.make_async_copy(
        merge_in.at[0, 0], merge_in.at[0, 0], merge_recv.at[0, 1 - core]
    ).wait()
    for r in others:
        for c in range(2):
            pltpu.make_async_copy(
                merge_in.at[c, r], merge_in.at[c, r], merge_recv.at[r, c]
            ).wait()

    low_row = low_lane[0:1]
    attended = []
    for c in range(2):
        shares = []
        for h in range(HEADS_HERE):
            tops = []
            for r in range(MEMBERS):
                rows = merge_in[c, r, folded:].astype(f32)
                tops.append(
                    rows[3 * h : 3 * h + 1]
                    + rows[3 * h + 1 : 3 * h + 2]
                    + rows[3 * h + 2 : 3 * h + 3]
                )
            top = functools.reduce(jnp.maximum, tops)
            weights = [jnp.exp(t - top) for t in tops]
            inverse = 1.0 / functools.reduce(jnp.add, weights)
            shares.append([w * inverse for w in weights])
        blocks = []
        for start, low_head, high_head in ((0, 0, 1), (32, 0, 2), (64, 1, 2)):
            total = jnp.zeros((32, TILE), f32)
            for r in range(MEMBERS):
                share = jnp.where(low_row, shares[low_head][r], shares[high_head][r])
                total += merge_in[c, r, start : start + 32].astype(f32) * share
            blocks.append(total)
        tokens = jnp.concatenate(blocks + [jnp.zeros((32, TILE), f32)], axis=0).T
        attended.append(
            (tokens[0:64, 0:folded].astype(bf16), tokens[64:128, 0:folded].astype(bf16))
        )
    part_width = partial.shape[3]

    def scatter(part, step):
        peer = (chip + step) % chips
        return pltpu.make_async_remote_copy(
            src_ref=partial.at[part, peer],
            dst_ref=parts.at[part, chip],
            send_sem=p_send.at[part],
            recv_sem=p_recv.at[part],
            device_id=(blk, 2 * peer + core),
            device_id_type=MESH,
        )

    own_parts = []
    for part in range(PARTS):
        cols = slice(part * part_width, (part + 1) * part_width)
        product = jnp.zeros((TILE // 2, part_width), f32)
        for c in range(2):
            for fold_at in range(2):
                rows = slice(fold_at * folded, (fold_at + 1) * folded)
                product += jnp.dot(
                    attended[c][fold_at], w_vmem[c, rows, cols], preferred_element_type=f32
                )
        partial[part] = product.reshape(chips, TILE // groups, part_width).astype(bf16)

        @pl.loop(1, chips)
        def _(step):
            scatter(part, step).start()

        own = pltpu.make_async_copy(
            partial.at[part, chip], parts.at[part, chip], p_own.at[part]
        )
        own.start()
        own_parts.append(own)

    for part in range(PARTS):
        own_parts[part].wait()
        arrived = parts.at[part, pl.ds(0, chips - 1)]
        pltpu.make_async_copy(arrived, arrived, p_recv.at[part]).wait()
        cols = slice(part * part_width, (part + 1) * part_width)
        summed = jnp.sum(parts[part].astype(f32), axis=0)
        out_ref[:, cols] = (summed * gate_ref[:, cols]).astype(bf16)

    pltpu.make_async_copy(all_kv, all_kv, kv_send).wait()
    pltpu.make_async_copy(all_q, all_q, q_send).wait()
    w_share.wait_send()
    swap.wait_send()
    for move in q_moves:
        move.wait_send()
    for merge in merges:
        merge.wait_send()
    for part in range(PARTS):
        sent = parts.at[part, pl.ds(0, chips - 1)]
        pltpu.make_async_copy(sent, sent, p_send.at[part]).wait()

    @pl.loop(1, far_step)
    def _(step):
        for piece in range(PIECES):
            link(UP, piece, step).wait_send()
            link(DOWN, piece, step).wait_send()

    for piece in (0, 1):
        link(UP, piece, far_step).wait_send()
    for piece in (2, 3):
        link(DOWN, piece, far_step).wait_send()


def body(query_rows, key_rows, value_rows, out_weight, out_gate, radial_mask, span_anchor):
    groups = lax.axis_size("head")
    span_z = lax.axis_size("blk") // 2
    ring = span_z // 2
    rows, width = query_rows.shape
    bf16, f32 = jnp.bfloat16, jnp.float32
    dma, vmem = pltpu.SemaphoreType.DMA, pltpu.VMEM
    steps = ring // 2 + 1
    return pl.pallas_call(
        functools.partial(kernel, groups, span_z),
        out_shape=jax.ShapeDtypeStruct((rows, width), bf16),
        in_specs=[pl.BlockSpec(memory_space=pl.ANY)] * 7,
        out_specs=pl.BlockSpec(memory_space=pltpu.VMEM),
        scratch_shapes=[
            pltpu.SMEM(span_anchor.shape, jnp.int32),
            pltpu.SMEM(radial_mask.shape, jnp.int32),
            vmem((1, width), f32),
            vmem((2, rows, width), bf16),
            vmem((MEMBERS, rows, width), bf16),
            vmem((groups, 2, rows, 256), bf16),
            vmem((groups, MEMBERS, rows, 256), bf16),
            vmem((ring, 2, WIDTH, TILE), bf16),
            vmem((2 * HEAD_DIM, 2 * QUERIES), bf16),
            vmem((2 * HEAD_DIM, 2 * QUERIES), bf16),
            vmem((HEADS_HERE, HEAD_DIM, QUERIES), f32),
            vmem((MEMBERS, 2, WIDTH // 2 + 16, TILE), bf16),
            vmem((2, MEMBERS, WIDTH // 2 + 16, TILE), bf16),
            vmem((2, WIDTH, width), bf16),
            vmem((PARTS, groups // 2, rows, width // PARTS), bf16),
            vmem((PARTS, groups // 2, rows, width // PARTS), bf16),
            dma((3,)),
            dma((3,)),
            dma,
            dma,
            dma,
            dma,
            dma,
            dma((2,)),
            dma,
            dma,
            dma((2, PIECES, steps)),
            dma((2, PIECES, steps)),
            dma((MEMBERS, 2)),
            dma((MEMBERS, 2)),
            dma((2 * MEMBERS,)),
            dma((PARTS,)),
            dma((PARTS,)),
            dma((PARTS,)),
        ],
        compiler_params=pltpu.CompilerParams(
            collective_id=0, has_side_effects=True, vmem_limit_bytes=56 * 1024 * 1024
        ),
        name="radial_attention",
    )(
        span_anchor,
        radial_mask,
        query_rows,
        key_rows,
        value_rows,
        out_weight,
        out_gate.reshape(1, width),
    )


def solution(mesh):
    return jax.shard_map(
        body,
        mesh=mesh,
        in_specs=(
            P(("blk", "head"), None),
            P(("blk", "head"), None),
            P(("blk", "head"), None),
            P("head", None),
            P(),
            P(),
            P(),
        ),
        out_specs=P(("blk", "head"), None),
        check_vma=False,
    )
```

```python
import functools

import jax
import jax.numpy as jnp
from jax import lax
from jax.experimental import pallas as pl
from jax.experimental.pallas import tpu as pltpu
from jax.sharding import PartitionSpec as P

MESH = pl.DeviceIdType.MESH
HEAD_DIM = 64
TILE = 128
HEADS_HERE = 3
WIDTH = HEADS_HERE * HEAD_DIM
LOW = -1e30
UP, DOWN = 0, 1
MEMBERS = 4
QUERIES = MEMBERS * TILE
PIECES = 4
PARTS = 4


def kernel(
    groups,
    span_z,
    anchor_hbm,
    mask_hbm,
    q_hbm,
    k_hbm,
    v_hbm,
    w_hbm,
    gate_hbm,
    out_ref,
    anchor_ref,
    mask_ref,
    gate_ref,
    stage,
    raw_q,
    in_kv,
    in_q,
    kv,
    weights01,
    weights2,
    acc,
    merge_out,
    merge_in,
    w_vmem,
    partial,
    parts,
    local_sem,
    small_sem,
    w_sem,
    kv_send,
    kv_recv,
    q_send,
    q_recv,
    own_sem,
    share_send,
    share_recv,
    ring_send,
    ring_recv,
    merge_send,
    merge_recv,
    core_sem,
    p_send,
    p_recv,
    p_own,
):
    f32, bf16 = jnp.float32, jnp.bfloat16
    blk = lax.axis_index("blk")
    me = lax.axis_index("head")
    half = blk // span_z
    z = blk % span_z
    parity = z % 2
    ring = span_z // 2
    place = z // 2
    base = half * span_z + parity
    core = me % 2
    chip = me // 2
    chips = groups // 2

    def blk_at(where):
        return base + 2 * where

    up_blk = blk_at((place + 1) % ring)
    down_blk = blk_at((place + ring - 1) % ring)

    def member_blk(r):
        other_half = (half + r // 2) % 2
        other_parity = (parity + r % 2) % 2
        return other_half * span_z + 2 * place + other_parity

    member_blks = [member_blk(r) for r in range(MEMBERS)]
    core_mate = 2 * chip + 1 - core

    loads = [
        pltpu.make_async_copy(src, stage.at[i] if i < 2 else raw_q.at[0], local_sem.at[i])
        for i, src in enumerate((k_hbm, v_hbm, q_hbm))
    ]
    for load in loads:
        load.start()
    w_load = pltpu.make_async_copy(w_hbm, w_vmem.at[core], w_sem)
    w_load.start()
    small_loads = [
        pltpu.make_async_copy(src, dst, small_sem.at[i])
        for i, (src, dst) in enumerate(
            ((anchor_hbm, anchor_ref), (mask_hbm, mask_ref), (gate_hbm, gate_ref))
        )
    ]
    for load in small_loads:
        load.start()

    barrier = pltpu.get_barrier_semaphore()

    @pl.loop(1, groups)
    def _(step):
        pl.semaphore_signal(
            barrier, inc=1, device_id=(blk, (me + step) % groups), device_id_type=MESH
        )

    greeted = [up_blk, down_blk] + member_blks[1:]
    for other in greeted:
        pl.semaphore_signal(barrier, inc=1, device_id=(other, me), device_id_type=MESH)
    for other in member_blks[1:]:
        pl.semaphore_signal(barrier, inc=1, device_id=(other, core_mate), device_id_type=MESH)
    pl.semaphore_wait(barrier, groups - 1 + len(greeted) + MEMBERS - 1)
    for load in loads:
        load.wait()

    def columns_of(group):
        return pl.ds(pl.multiple_of((group // 2) * (2 * WIDTH) + (group % 2) * 128, 128), 256)

    slot = core * chips + chip

    def exchange_kv(step):
        peer = (me + step) % groups
        return pltpu.make_async_remote_copy(
            src_ref=stage.at[:, :, columns_of(peer)],
            dst_ref=in_kv.at[slot],
            send_sem=kv_send,
            recv_sem=kv_recv,
            device_id=(blk, peer),
            device_id_type=MESH,
        )

    def exchange_q(step):
        peer = (me + step) % groups
        return pltpu.make_async_remote_copy(
            src_ref=raw_q.at[:, :, columns_of(peer)],
            dst_ref=in_q.at[slot],
            send_sem=q_send,
            recv_sem=q_recv,
            device_id=(blk, peer),
            device_id_type=MESH,
        )

    @pl.loop(1, groups)
    def _(step):
        exchange_kv(step).start()

    def to_member(r, src, dst, send, recv):
        return pltpu.make_async_remote_copy(
            src_ref=src,
            dst_ref=dst,
            send_sem=send,
            recv_sem=recv,
            device_id=(member_blks[r], me),
            device_id_type=MESH,
        )

    others = (3, 1, 2)
    q_moves = [
        to_member(r, raw_q.at[0], raw_q.at[r], core_sem.at[r], core_sem.at[MEMBERS + r])
        for r in others
    ]
    for move in q_moves:
        move.start()

    own_kv = pltpu.make_async_copy(
        stage.at[:, :, columns_of(me)], in_kv.at[slot], own_sem.at[0]
    )
    own_kv.start()
    w_load.wait()
    w_share = pltpu.make_async_remote_copy(
        src_ref=w_vmem.at[core],
        dst_ref=w_vmem.at[core],
        send_sem=share_send,
        recv_sem=share_recv,
        device_id=(blk, core_mate),
        device_id_type=MESH,
    )
    w_share.start()
    own_kv.wait()
    all_kv = in_kv.at[pl.ds(0, groups - 1)]
    all_q = in_q.at[pl.ds(0, groups - 1)]
    pltpu.make_async_copy(all_kv, all_kv, kv_recv).wait()

    lane = lax.broadcasted_iota(jnp.int32, (TILE, 128), 1)
    low_lane = lane < 64
    odd = jnp.full((TILE, 128), core, jnp.int32) == 1

    def aligned(rows):
        rows = rows.astype(f32).reshape(TILE, 256)
        first, second = rows[:, 0:128], rows[:, 128:256]
        first_r, second_r = pltpu.roll(first, 64, 1), pltpu.roll(second, 64, 1)
        a = jnp.where(odd, jnp.where(low_lane, first_r, second_r), first)
        b = jnp.where(odd, second_r, second)
        return a, b

    def link(direction, piece, step):
        where = (place + ring - (step - 1)) % ring if direction == UP else (place + step - 1) % ring
        block = kv.at[where, piece // 2, pl.ds((piece % 2) * (WIDTH // 2), WIDTH // 2)]
        return pltpu.make_async_remote_copy(
            src_ref=block,
            dst_ref=block,
            send_sem=ring_send.at[direction, piece, step],
            recv_sem=ring_recv.at[direction, piece, step],
            device_id=(up_blk if direction == UP else down_blk, me),
            device_id_type=MESH,
        )

    far_step = ring // 2

    def piece_at(direction, turn):
        return turn if direction == UP else (turn + PIECES // 2) % PIECES

    def pass_on(step):
        for turn in range(PIECES):
            for direction in (UP, DOWN):
                piece = piece_at(direction, turn)
                link(direction, piece, step).wait_recv()
                if (piece < 2) == (direction == UP):
                    link(direction, piece, step + 1).start()
                else:

                    @pl.when(step < far_step - 1)
                    def _():
                        link(direction, piece, step + 1).start()

    k_a, k_b = aligned(in_kv[:, 0])
    kv[place, 0, 0:TILE] = k_a.astype(bf16)
    kv[place, 0, TILE:WIDTH] = jnp.where(
        low_lane[0:64], k_b[0:64], pltpu.roll(k_b[64:128], 64, 1)
    ).astype(bf16)
    for piece in (0, 1):
        link(UP, piece, 1).start()
    v_a, v_b = aligned(in_kv[:, 1])
    kv[place, 1, 0:128] = v_a.T.astype(bf16)
    kv[place, 1, 128:WIDTH] = v_b.T[0:64].astype(bf16)
    for piece in (2, 3):
        link(DOWN, piece, 1).start()
    for turn in (2, 3):
        link(UP, piece_at(UP, turn), 1).start()
        link(DOWN, piece_at(DOWN, turn), 1).start()
    for move in q_moves:
        move.wait_recv()

    @pl.loop(1, groups)
    def _(step):
        exchange_q(step).start()

    own_q = pltpu.make_async_copy(raw_q.at[:, :, columns_of(me)], in_q.at[slot], own_sem.at[1])
    own_q.start()
    weights01[...] = jnp.zeros_like(weights01)
    weights2[...] = jnp.zeros_like(weights2)
    acc[...] = jnp.zeros_like(acc)
    for load in small_loads:
        load.wait()
    anchors = [anchor_ref[member_blks[r]] for r in range(MEMBERS)]
    pass_on(1)
    own_q.wait()
    pltpu.make_async_copy(all_q, all_q, q_recv).wait()
    scale = HEAD_DIM ** (-0.5)
    for r in range(MEMBERS):
        q_a, q_b = aligned(in_q[:, r])
        top_q = (q_a.T * scale).astype(bf16)
        last_q = (q_b.T[0:64] * scale).astype(bf16)
        cols = slice(r * TILE, (r + 1) * TILE)
        far = slice(QUERIES + r * TILE, QUERIES + (r + 1) * TILE)
        weights01[0:64, cols] = top_q[0:64]
        weights01[64:128, far] = top_q[64:128]
        weights2[0:64, cols] = last_q
        weights2[64:128, far] = last_q

    def bias_of(where):
        anchor = anchor_ref[blk_at(where)]
        return jnp.concatenate(
            [
                jnp.full(
                    (1, TILE), jnp.where(mask_ref[anchors[r], anchor] > 0, f32(0.0), f32(LOW)), f32
                )
                for r in range(MEMBERS)
            ],
            axis=1,
        )

    def scores_of(where):
        bias = bias_of(where)
        two = jnp.dot(kv[where, 0, 0:TILE], weights01[...], preferred_element_type=f32)
        one = jnp.dot(kv[where, 0, TILE:WIDTH], weights2[...], preferred_element_type=f32)
        third = jnp.concatenate([one[:, 0:QUERIES], one[:, QUERIES:]], axis=0)
        return two[:, 0:QUERIES] + bias, two[:, QUERIES:] + bias, third + bias

    def soften(tiles, state):
        maxima, sums = state
        scores = [scores_of(where) for where in tiles]
        new_max, new_sum, probs, scales = [], [], [], []
        for h in range(HEADS_HERE):
            here = [s[h] for s in scores]
            top = maxima[h]
            for s in here:
                top = jnp.maximum(top, jnp.max(s, axis=0, keepdims=True))
            weights = [jnp.exp(s - top) for s in here]
            fade = jnp.exp(maxima[h] - top)
            total = sums[h] * fade
            for w in weights:
                total = total + jnp.sum(w, axis=0, keepdims=True)
            new_max.append(top)
            new_sum.append(total)
            scales.append(fade)
            probs.append([w.astype(bf16) for w in weights])
        return (tuple(new_max), tuple(new_sum)), probs, scales

    def gather_values(tiles, probs, scales):
        for h in range(HEADS_HERE):
            rows = slice(h * HEAD_DIM, (h + 1) * HEAD_DIM)
            if len(tiles) == 1:
                values, weights = kv[tiles[0], 1, rows], probs[h][0]
            else:
                values = jnp.concatenate([kv[t, 1, rows] for t in tiles], axis=1)
                weights = jnp.concatenate(probs[h], axis=0)
            acc[h] = acc[h] * scales[h] + jnp.dot(values, weights, preferred_element_type=f32)

    empty_max = jnp.full((1, QUERIES), LOW, f32)
    empty_sum = jnp.zeros((1, QUERIES), f32)
    state = ((empty_max,) * HEADS_HERE, (empty_sum,) * HEADS_HERE)
    state, probs, scales = soften([place], state)
    gather_values([place], probs, scales)

    def compute_pair(step, state):
        tiles = [(place + ring - step) % ring, (place + step) % ring]
        state, probs, scales = soften(tiles, state)
        gather_values(tiles, probs, scales)
        return state

    def ring_step(step, state):
        pass_on(step)
        return compute_pair(step - 1, state)

    state = lax.fori_loop(2, far_step, ring_step, state)
    state = compute_pair(far_step - 1, state)
    last = (place + far_step) % ring
    for piece in (0, 1):
        link(UP, piece, far_step).wait_recv()
    state, probs, scales = soften([last], state)
    for piece in (2, 3):
        link(DOWN, piece, far_step).wait_recv()
    gather_values([last], probs, scales)
    maxima, sums = state

    def split_level(level):
        high = level.astype(bf16).astype(f32)
        middle = (level - high).astype(bf16).astype(f32)
        return [high, middle, level - high - middle]

    levels = [row for h in range(HEADS_HERE) for row in split_level(maxima[h] + jnp.log(sums[h]))]
    levels = jnp.concatenate(levels + [jnp.zeros((16 - len(levels), QUERIES), f32)], axis=0)
    folded = WIDTH // 2
    low16, low_f = low_lane[0:16], low_lane[0:folded]

    def fold(r):
        lanes = slice(r * TILE, (r + 1) * TILE)
        value = jnp.concatenate(
            [acc[h, :, lanes] * (1.0 / sums[h][:, lanes]) for h in range(HEADS_HERE)], axis=0
        )
        upper, lower = value[0:folded], value[folded:WIDTH]
        level = levels[:, lanes]
        level_r = pltpu.roll(level, 64, 1)
        merge_out[r, 0, 0:folded] = jnp.where(low_f, upper, pltpu.roll(lower, 64, 1)).astype(bf16)
        merge_out[r, 1, 0:folded] = jnp.where(low_f, pltpu.roll(upper, 64, 1), lower).astype(bf16)
        merge_out[r, 0, folded:] = jnp.where(low16, level, level_r).astype(bf16)
        merge_out[r, 1, folded:] = jnp.where(low16, level_r, level).astype(bf16)

    merges = []
    for r in others:
        fold(r)
        for c in range(2):
            merge = pltpu.make_async_remote_copy(
                src_ref=merge_out.at[r, c],
                dst_ref=merge_in.at[core, r],
                send_sem=merge_send.at[r, c],
                recv_sem=merge_recv.at[r, core],
                device_id=(member_blks[r], 2 * chip + c),
                device_id_type=MESH,
            )
            merge.start()
            merges.append(merge)
    fold(0)
    swap = pltpu.make_async_remote_copy(
        src_ref=merge_out.at[0, 1 - core],
        dst_ref=merge_in.at[core, 0],
        send_sem=merge_send.at[0, 0],
        recv_sem=merge_recv.at[0, core],
        device_id=(blk, core_mate),
        device_id_type=MESH,
    )
    swap.start()
    merge_in[core, 0] = merge_out[0, core]
    w_share.wait_recv()
    pltpu.make_async_copy(
        merge_in.at[0, 0], merge_in.at[0, 0], merge_recv.at[0, 1 - core]
    ).wait()
    for r in others:
        for c in range(2):
            pltpu.make_async_copy(
                merge_in.at[c, r], merge_in.at[c, r], merge_recv.at[r, c]
            ).wait()

    low_row = low_lane[0:1]
    attended = []
    for c in range(2):
        shares = []
        for h in range(HEADS_HERE):
            tops = []
            for r in range(MEMBERS):
                rows = merge_in[c, r, folded:].astype(f32)
                tops.append(
                    rows[3 * h : 3 * h + 1]
                    + rows[3 * h + 1 : 3 * h + 2]
                    + rows[3 * h + 2 : 3 * h + 3]
                )
            top = functools.reduce(jnp.maximum, tops)
            weights = [jnp.exp(t - top) for t in tops]
            inverse = 1.0 / functools.reduce(jnp.add, weights)
            shares.append([w * inverse for w in weights])
        blocks = []
        for start, low_head, high_head in ((0, 0, 1), (32, 0, 2), (64, 1, 2)):
            total = jnp.zeros((32, TILE), f32)
            for r in range(MEMBERS):
                share = jnp.where(low_row, shares[low_head][r], shares[high_head][r])
                total += merge_in[c, r, start : start + 32].astype(f32) * share
            blocks.append(total)
        tokens = jnp.concatenate(blocks + [jnp.zeros((32, TILE), f32)], axis=0).T
        attended.append(
            (tokens[0:64, 0:folded].astype(bf16), tokens[64:128, 0:folded].astype(bf16))
        )
    part_width = partial.shape[3]

    def scatter(part, step):
        peer = (chip + step) % chips
        return pltpu.make_async_remote_copy(
            src_ref=partial.at[part, peer],
            dst_ref=parts.at[part, chip],
            send_sem=p_send.at[part],
            recv_sem=p_recv.at[part],
            device_id=(blk, 2 * peer + core),
            device_id_type=MESH,
        )

    own_parts = []
    for part in range(PARTS):
        cols = slice(part * part_width, (part + 1) * part_width)
        product = jnp.zeros((TILE // 2, part_width), f32)
        for c in range(2):
            for fold_at in range(2):
                rows = slice(fold_at * folded, (fold_at + 1) * folded)
                product += jnp.dot(
                    attended[c][fold_at], w_vmem[c, rows, cols], preferred_element_type=f32
                )
        partial[part] = product.reshape(chips, TILE // groups, part_width).astype(bf16)

        @pl.loop(1, chips)
        def _(step):
            scatter(part, step).start()

        own = pltpu.make_async_copy(
            partial.at[part, chip], parts.at[part, chip], p_own.at[part]
        )
        own.start()
        own_parts.append(own)

    for part in range(PARTS):
        own_parts[part].wait()
        arrived = parts.at[part, pl.ds(0, chips - 1)]
        pltpu.make_async_copy(arrived, arrived, p_recv.at[part]).wait()
        cols = slice(part * part_width, (part + 1) * part_width)
        summed = jnp.sum(parts[part].astype(f32), axis=0)
        out_ref[:, cols] = (summed * gate_ref[:, cols]).astype(bf16)

    pltpu.make_async_copy(all_kv, all_kv, kv_send).wait()
    pltpu.make_async_copy(all_q, all_q, q_send).wait()
    w_share.wait_send()
    swap.wait_send()
    for move in q_moves:
        move.wait_send()
    for merge in merges:
        merge.wait_send()
    for part in range(PARTS):
        sent = parts.at[part, pl.ds(0, chips - 1)]
        pltpu.make_async_copy(sent, sent, p_send.at[part]).wait()

    @pl.loop(1, far_step)
    def _(step):
        for piece in range(PIECES):
            link(UP, piece, step).wait_send()
            link(DOWN, piece, step).wait_send()

    for piece in (0, 1):
        link(UP, piece, far_step).wait_send()
    for piece in (2, 3):
        link(DOWN, piece, far_step).wait_send()


def body(query_rows, key_rows, value_rows, out_weight, out_gate, radial_mask, span_anchor):
    groups = lax.axis_size("head")
    span_z = lax.axis_size("blk") // 2
    ring = span_z // 2
    rows, width = query_rows.shape
    bf16, f32 = jnp.bfloat16, jnp.float32
    dma, vmem = pltpu.SemaphoreType.DMA, pltpu.VMEM
    steps = ring // 2 + 1
    return pl.pallas_call(
        functools.partial(kernel, groups, span_z),
        out_shape=jax.ShapeDtypeStruct((rows, width), bf16),
        in_specs=[pl.BlockSpec(memory_space=pltpu.HBM)] * 7,
        out_specs=pl.BlockSpec(memory_space=pltpu.VMEM),
        scratch_shapes=[
            pltpu.SMEM(span_anchor.shape, jnp.int32),
            pltpu.SMEM(radial_mask.shape, jnp.int32),
            vmem((1, width), f32),
            vmem((2, rows, width), bf16),
            vmem((MEMBERS, rows, width), bf16),
            vmem((groups, 2, rows, 256), bf16),
            vmem((groups, MEMBERS, rows, 256), bf16),
            vmem((ring, 2, WIDTH, TILE), bf16),
            vmem((2 * HEAD_DIM, 2 * QUERIES), bf16),
            vmem((2 * HEAD_DIM, 2 * QUERIES), bf16),
            vmem((HEADS_HERE, HEAD_DIM, QUERIES), f32),
            vmem((MEMBERS, 2, WIDTH // 2 + 16, TILE), bf16),
            vmem((2, MEMBERS, WIDTH // 2 + 16, TILE), bf16),
            vmem((2, WIDTH, width), bf16),
            vmem((PARTS, groups // 2, rows, width // PARTS), bf16),
            vmem((PARTS, groups // 2, rows, width // PARTS), bf16),
            dma((3,)),
            dma((3,)),
            dma,
            dma,
            dma,
            dma,
            dma,
            dma((2,)),
            dma,
            dma,
            dma((2, PIECES, steps)),
            dma((2, PIECES, steps)),
            dma((MEMBERS, 2)),
            dma((MEMBERS, 2)),
            dma((2 * MEMBERS,)),
            dma((PARTS,)),
            dma((PARTS,)),
            dma((PARTS,)),
        ],
        compiler_params=pltpu.CompilerParams(
            collective_id=0, has_side_effects=True, vmem_limit_bytes=48000 * 1024
        ),
        name="radial_attention",
    )(
        *[
            pltpu.with_memory_space_constraint(x, pltpu.HBM)
            for x in (
                span_anchor,
                radial_mask,
                query_rows,
                key_rows,
                value_rows,
                out_weight,
                out_gate.reshape(1, width),
            )
        ]
    )


def solution(mesh):
    return jax.shard_map(
        body,
        mesh=mesh,
        in_specs=(
            P(("blk", "head"), None),
            P(("blk", "head"), None),
            P(("blk", "head"), None),
            P("head", None),
            P(),
            P(),
            P(),
        ),
        out_specs=P(("blk", "head"), None),
        check_vma=False,
    )
```

```python
import functools

import jax
import jax.numpy as jnp
from jax import lax
from jax.experimental import pallas as pl
from jax.experimental.pallas import tpu as pltpu
from jax.sharding import PartitionSpec as P

MESH = pl.DeviceIdType.MESH
HEAD_DIM = 64
TILE = 128
HEADS_HERE = 3
WIDTH = HEADS_HERE * HEAD_DIM
LOW = -1e30
UP, DOWN = 0, 1
MEMBERS = 4
QUERIES = MEMBERS * TILE
PIECES = 4
PARTS = 4


def kernel(
    groups,
    span_z,
    anchor_hbm,
    mask_hbm,
    q_hbm,
    k_hbm,
    v_hbm,
    w_hbm,
    gate_hbm,
    out_ref,
    anchor_ref,
    mask_ref,
    gate_ref,
    stage,
    raw_q,
    in_kv,
    in_q,
    kv,
    weights01,
    weights2,
    acc,
    merge_out,
    merge_in,
    w_vmem,
    partial,
    parts,
    local_sem,
    small_sem,
    w_sem,
    kv_send,
    kv_recv,
    q_send,
    q_recv,
    own_sem,
    share_send,
    share_recv,
    ring_send,
    ring_recv,
    merge_send,
    merge_recv,
    core_sem,
    p_send,
    p_recv,
    p_own,
):
    f32, bf16 = jnp.float32, jnp.bfloat16
    blk = lax.axis_index("blk")
    me = lax.axis_index("head")
    half = blk // span_z
    z = blk % span_z
    parity = z % 2
    ring = span_z // 2
    place = z // 2
    base = half * span_z + parity
    core = me % 2
    chip = me // 2
    chips = groups // 2

    def blk_at(where):
        return base + 2 * where

    up_blk = blk_at((place + 1) % ring)
    down_blk = blk_at((place + ring - 1) % ring)

    def member_blk(r):
        other_half = (half + r // 2) % 2
        other_parity = (parity + r % 2) % 2
        return other_half * span_z + 2 * place + other_parity

    member_blks = [member_blk(r) for r in range(MEMBERS)]
    core_mate = 2 * chip + 1 - core

    loads = [
        pltpu.make_async_copy(src, stage.at[i] if i < 2 else raw_q.at[0], local_sem.at[i])
        for i, src in enumerate((k_hbm, v_hbm, q_hbm))
    ]
    for load in loads[0:2]:
        load.start()
    w_load = pltpu.make_async_copy(w_hbm, w_vmem.at[core], w_sem)
    small_loads = [
        pltpu.make_async_copy(src, dst, small_sem.at[i])
        for i, (src, dst) in enumerate(
            ((anchor_hbm, anchor_ref), (mask_hbm, mask_ref), (gate_hbm, gate_ref))
        )
    ]

    barrier = pltpu.get_barrier_semaphore()

    @pl.loop(1, groups)
    def _(step):
        pl.semaphore_signal(
            barrier, inc=1, device_id=(blk, (me + step) % groups), device_id_type=MESH
        )

    greeted = [up_blk, down_blk] + member_blks[1:]
    for other in greeted:
        pl.semaphore_signal(barrier, inc=1, device_id=(other, me), device_id_type=MESH)
    for other in member_blks[1:]:
        pl.semaphore_signal(barrier, inc=1, device_id=(other, core_mate), device_id_type=MESH)
    loads[2].start()
    w_load.start()
    for load in small_loads:
        load.start()
    pl.semaphore_wait(barrier, groups - 1 + len(greeted) + MEMBERS - 1)
    for load in loads:
        load.wait()

    def columns_of(group):
        return pl.ds(pl.multiple_of((group // 2) * (2 * WIDTH) + (group % 2) * 128, 128), 256)

    slot = core * chips + chip

    def exchange_kv(step):
        peer = (me + step) % groups
        return pltpu.make_async_remote_copy(
            src_ref=stage.at[:, :, columns_of(peer)],
            dst_ref=in_kv.at[slot],
            send_sem=kv_send,
            recv_sem=kv_recv,
            device_id=(blk, peer),
            device_id_type=MESH,
        )

    def exchange_q(step):
        peer = (me + step) % groups
        return pltpu.make_async_remote_copy(
            src_ref=raw_q.at[:, :, columns_of(peer)],
            dst_ref=in_q.at[slot],
            send_sem=q_send,
            recv_sem=q_recv,
            device_id=(blk, peer),
            device_id_type=MESH,
        )

    @pl.loop(1, groups)
    def _(step):
        exchange_kv(step).start()

    def to_member(r, src, dst, send, recv):
        return pltpu.make_async_remote_copy(
            src_ref=src,
            dst_ref=dst,
            send_sem=send,
            recv_sem=recv,
            device_id=(member_blks[r], me),
            device_id_type=MESH,
        )

    others = (3, 1, 2)
    q_moves = [
        to_member(r, raw_q.at[0], raw_q.at[r], core_sem.at[r], core_sem.at[MEMBERS + r])
        for r in others
    ]
    for move in q_moves:
        move.start()

    own_kv = pltpu.make_async_copy(
        stage.at[:, :, columns_of(me)], in_kv.at[slot], own_sem.at[0]
    )
    own_kv.start()
    w_load.wait()
    w_share = pltpu.make_async_remote_copy(
        src_ref=w_vmem.at[core],
        dst_ref=w_vmem.at[core],
        send_sem=share_send,
        recv_sem=share_recv,
        device_id=(blk, core_mate),
        device_id_type=MESH,
    )
    w_share.start()
    own_kv.wait()
    all_kv = in_kv.at[pl.ds(0, groups - 1)]
    all_q = in_q.at[pl.ds(0, groups - 1)]
    pltpu.make_async_copy(all_kv, all_kv, kv_recv).wait()

    lane = lax.broadcasted_iota(jnp.int32, (TILE, 128), 1)
    low_lane = lane < 64
    odd = jnp.full((TILE, 128), core, jnp.int32) == 1

    def aligned(rows):
        rows = rows.astype(f32).reshape(TILE, 256)
        first, second = rows[:, 0:128], rows[:, 128:256]
        first_r, second_r = pltpu.roll(first, 64, 1), pltpu.roll(second, 64, 1)
        a = jnp.where(odd, jnp.where(low_lane, first_r, second_r), first)
        b = jnp.where(odd, second_r, second)
        return a, b

    def link(direction, piece, step):
        where = (place + ring - (step - 1)) % ring if direction == UP else (place + step - 1) % ring
        block = kv.at[where, piece // 2, pl.ds((piece % 2) * (WIDTH // 2), WIDTH // 2)]
        return pltpu.make_async_remote_copy(
            src_ref=block,
            dst_ref=block,
            send_sem=ring_send.at[direction, piece, step],
            recv_sem=ring_recv.at[direction, piece, step],
            device_id=(up_blk if direction == UP else down_blk, me),
            device_id_type=MESH,
        )

    far_step = ring // 2

    def piece_at(direction, turn):
        return turn if direction == UP else (turn + PIECES // 2) % PIECES

    def pass_on(step):
        for turn in range(PIECES):
            for direction in (UP, DOWN):
                piece = piece_at(direction, turn)
                link(direction, piece, step).wait_recv()
                if (piece < 2) == (direction == UP):
                    link(direction, piece, step + 1).start()
                else:

                    @pl.when(step < far_step - 1)
                    def _():
                        link(direction, piece, step + 1).start()

    k_a, k_b = aligned(in_kv[:, 0])
    kv[place, 0, 0:TILE] = k_a.astype(bf16)
    kv[place, 0, TILE:WIDTH] = jnp.where(
        low_lane[0:64], k_b[0:64], pltpu.roll(k_b[64:128], 64, 1)
    ).astype(bf16)
    for piece in (0, 1):
        link(UP, piece, 1).start()
    v_a, v_b = aligned(in_kv[:, 1])
    kv[place, 1, 0:128] = v_a.T.astype(bf16)
    kv[place, 1, 128:WIDTH] = v_b.T[0:64].astype(bf16)
    for piece in (2, 3):
        link(DOWN, piece, 1).start()
    for turn in (2, 3):
        link(UP, piece_at(UP, turn), 1).start()
        link(DOWN, piece_at(DOWN, turn), 1).start()
    for move in q_moves:
        move.wait_recv()

    @pl.loop(1, groups)
    def _(step):
        exchange_q(step).start()

    own_q = pltpu.make_async_copy(raw_q.at[:, :, columns_of(me)], in_q.at[slot], own_sem.at[1])
    own_q.start()
    weights01[...] = jnp.zeros_like(weights01)
    weights2[...] = jnp.zeros_like(weights2)
    acc[...] = jnp.zeros_like(acc)
    for load in small_loads:
        load.wait()
    anchors = [anchor_ref[member_blks[r]] for r in range(MEMBERS)]
    pass_on(1)
    own_q.wait()
    pltpu.make_async_copy(all_q, all_q, q_recv).wait()
    scale = HEAD_DIM ** (-0.5)
    for r in range(MEMBERS):
        q_a, q_b = aligned(in_q[:, r])
        top_q = (q_a.T * scale).astype(bf16)
        last_q = (q_b.T[0:64] * scale).astype(bf16)
        cols = slice(r * TILE, (r + 1) * TILE)
        far = slice(QUERIES + r * TILE, QUERIES + (r + 1) * TILE)
        weights01[0:64, cols] = top_q[0:64]
        weights01[64:128, far] = top_q[64:128]
        weights2[0:64, cols] = last_q
        weights2[64:128, far] = last_q

    def bias_of(where):
        anchor = anchor_ref[blk_at(where)]
        return jnp.concatenate(
            [
                jnp.full(
                    (1, TILE), jnp.where(mask_ref[anchors[r], anchor] > 0, f32(0.0), f32(LOW)), f32
                )
                for r in range(MEMBERS)
            ],
            axis=1,
        )

    def scores_of(where):
        bias = bias_of(where)
        two = jnp.dot(kv[where, 0, 0:TILE], weights01[...], preferred_element_type=f32)
        one = jnp.dot(kv[where, 0, TILE:WIDTH], weights2[...], preferred_element_type=f32)
        third = jnp.concatenate([one[:, 0:QUERIES], one[:, QUERIES:]], axis=0)
        return two[:, 0:QUERIES] + bias, two[:, QUERIES:] + bias, third + bias

    def soften(tiles, state):
        maxima, sums = state
        scores = [scores_of(where) for where in tiles]
        new_max, new_sum, probs, scales = [], [], [], []
        for h in range(HEADS_HERE):
            here = [s[h] for s in scores]
            top = maxima[h]
            for s in here:
                top = jnp.maximum(top, jnp.max(s, axis=0, keepdims=True))
            weights = [jnp.exp(s - top) for s in here]
            fade = jnp.exp(maxima[h] - top)
            total = sums[h] * fade
            for w in weights:
                total = total + jnp.sum(w, axis=0, keepdims=True)
            new_max.append(top)
            new_sum.append(total)
            scales.append(fade)
            probs.append([w.astype(bf16) for w in weights])
        return (tuple(new_max), tuple(new_sum)), probs, scales

    def gather_values(tiles, probs, scales):
        for h in range(HEADS_HERE):
            rows = slice(h * HEAD_DIM, (h + 1) * HEAD_DIM)
            if len(tiles) == 1:
                values, weights = kv[tiles[0], 1, rows], probs[h][0]
            else:
                values = jnp.concatenate([kv[t, 1, rows] for t in tiles], axis=1)
                weights = jnp.concatenate(probs[h], axis=0)
            acc[h] = acc[h] * scales[h] + jnp.dot(values, weights, preferred_element_type=f32)

    empty_max = jnp.full((1, QUERIES), LOW, f32)
    empty_sum = jnp.zeros((1, QUERIES), f32)
    state = ((empty_max,) * HEADS_HERE, (empty_sum,) * HEADS_HERE)
    state, probs, scales = soften([place], state)
    gather_values([place], probs, scales)

    def compute_pair(step, state):
        tiles = [(place + ring - step) % ring, (place + step) % ring]
        state, probs, scales = soften(tiles, state)
        gather_values(tiles, probs, scales)
        return state

    def ring_step(step, state):
        pass_on(step)
        return compute_pair(step - 1, state)

    state = lax.fori_loop(2, far_step, ring_step, state)
    state = compute_pair(far_step - 1, state)
    last = (place + far_step) % ring
    for piece in (0, 1):
        link(UP, piece, far_step).wait_recv()
    state, probs, scales = soften([last], state)
    for piece in (2, 3):
        link(DOWN, piece, far_step).wait_recv()
    gather_values([last], probs, scales)
    maxima, sums = state

    def split_level(level):
        high = level.astype(bf16).astype(f32)
        middle = (level - high).astype(bf16).astype(f32)
        return [high, middle, level - high - middle]

    levels = [row for h in range(HEADS_HERE) for row in split_level(maxima[h] + jnp.log(sums[h]))]
    levels = jnp.concatenate(levels + [jnp.zeros((16 - len(levels), QUERIES), f32)], axis=0)
    folded = WIDTH // 2
    low16, low_f = low_lane[0:16], low_lane[0:folded]

    def fold(r):
        lanes = slice(r * TILE, (r + 1) * TILE)
        value = jnp.concatenate(
            [acc[h, :, lanes] * (1.0 / sums[h][:, lanes]) for h in range(HEADS_HERE)], axis=0
        )
        upper, lower = value[0:folded], value[folded:WIDTH]
        level = levels[:, lanes]
        level_r = pltpu.roll(level, 64, 1)
        merge_out[r, 0, 0:folded] = jnp.where(low_f, upper, pltpu.roll(lower, 64, 1)).astype(bf16)
        merge_out[r, 1, 0:folded] = jnp.where(low_f, pltpu.roll(upper, 64, 1), lower).astype(bf16)
        merge_out[r, 0, folded:] = jnp.where(low16, level, level_r).astype(bf16)
        merge_out[r, 1, folded:] = jnp.where(low16, level_r, level).astype(bf16)

    merges = []
    for r in others:
        fold(r)
        for c in range(2):
            merge = pltpu.make_async_remote_copy(
                src_ref=merge_out.at[r, c],
                dst_ref=merge_in.at[core, r],
                send_sem=merge_send.at[r, c],
                recv_sem=merge_recv.at[r, core],
                device_id=(member_blks[r], 2 * chip + c),
                device_id_type=MESH,
            )
            merge.start()
            merges.append(merge)
    fold(0)
    swap = pltpu.make_async_remote_copy(
        src_ref=merge_out.at[0, 1 - core],
        dst_ref=merge_in.at[core, 0],
        send_sem=merge_send.at[0, 0],
        recv_sem=merge_recv.at[0, core],
        device_id=(blk, core_mate),
        device_id_type=MESH,
    )
    swap.start()
    merge_in[core, 0] = merge_out[0, core]
    w_share.wait_recv()
    pltpu.make_async_copy(
        merge_in.at[0, 0], merge_in.at[0, 0], merge_recv.at[0, 1 - core]
    ).wait()
    for r in others:
        for c in range(2):
            pltpu.make_async_copy(
                merge_in.at[c, r], merge_in.at[c, r], merge_recv.at[r, c]
            ).wait()

    low_row = low_lane[0:1]
    attended = []
    for c in range(2):
        shares = []
        for h in range(HEADS_HERE):
            tops = []
            for r in range(MEMBERS):
                rows = merge_in[c, r, folded:].astype(f32)
                tops.append(
                    rows[3 * h : 3 * h + 1]
                    + rows[3 * h + 1 : 3 * h + 2]
                    + rows[3 * h + 2 : 3 * h + 3]
                )
            top = functools.reduce(jnp.maximum, tops)
            weights = [jnp.exp(t - top) for t in tops]
            inverse = 1.0 / functools.reduce(jnp.add, weights)
            shares.append([w * inverse for w in weights])
        blocks = []
        for start, low_head, high_head in ((0, 0, 1), (32, 0, 2), (64, 1, 2)):
            total = jnp.zeros((32, TILE), f32)
            for r in range(MEMBERS):
                share = jnp.where(low_row, shares[low_head][r], shares[high_head][r])
                total += merge_in[c, r, start : start + 32].astype(f32) * share
            blocks.append(total)
        tokens = jnp.concatenate(blocks + [jnp.zeros((32, TILE), f32)], axis=0).T
        attended.append(
            (tokens[0:64, 0:folded].astype(bf16), tokens[64:128, 0:folded].astype(bf16))
        )
    part_width = partial.shape[3]

    def scatter(part, step):
        peer = (chip + step) % chips
        return pltpu.make_async_remote_copy(
            src_ref=partial.at[part, peer],
            dst_ref=parts.at[part, chip],
            send_sem=p_send.at[part],
            recv_sem=p_recv.at[part],
            device_id=(blk, 2 * peer + core),
            device_id_type=MESH,
        )

    own_parts = []
    for part in range(PARTS):
        cols = slice(part * part_width, (part + 1) * part_width)
        product = jnp.zeros((TILE // 2, part_width), f32)
        for c in range(2):
            for fold_at in range(2):
                rows = slice(fold_at * folded, (fold_at + 1) * folded)
                product += jnp.dot(
                    attended[c][fold_at], w_vmem[c, rows, cols], preferred_element_type=f32
                )
        partial[part] = product.reshape(chips, TILE // groups, part_width).astype(bf16)

        @pl.loop(1, chips)
        def _(step):
            scatter(part, step).start()

        own = pltpu.make_async_copy(
            partial.at[part, chip], parts.at[part, chip], p_own.at[part]
        )
        own.start()
        own_parts.append(own)

    for part in range(PARTS):
        own_parts[part].wait()
        arrived = parts.at[part, pl.ds(0, chips - 1)]
        pltpu.make_async_copy(arrived, arrived, p_recv.at[part]).wait()
        cols = slice(part * part_width, (part + 1) * part_width)
        summed = jnp.sum(parts[part].astype(f32), axis=0)
        out_ref[:, cols] = (summed * gate_ref[:, cols]).astype(bf16)

    pltpu.make_async_copy(all_kv, all_kv, kv_send).wait()
    pltpu.make_async_copy(all_q, all_q, q_send).wait()
    w_share.wait_send()
    swap.wait_send()
    for move in q_moves:
        move.wait_send()
    for merge in merges:
        merge.wait_send()
    for part in range(PARTS):
        sent = parts.at[part, pl.ds(0, chips - 1)]
        pltpu.make_async_copy(sent, sent, p_send.at[part]).wait()

    @pl.loop(1, far_step)
    def _(step):
        for piece in range(PIECES):
            link(UP, piece, step).wait_send()
            link(DOWN, piece, step).wait_send()

    for piece in (0, 1):
        link(UP, piece, far_step).wait_send()
    for piece in (2, 3):
        link(DOWN, piece, far_step).wait_send()


def body(query_rows, key_rows, value_rows, out_weight, out_gate, radial_mask, span_anchor):
    groups = lax.axis_size("head")
    span_z = lax.axis_size("blk") // 2
    ring = span_z // 2
    rows, width = query_rows.shape
    bf16, f32 = jnp.bfloat16, jnp.float32
    dma, vmem = pltpu.SemaphoreType.DMA, pltpu.VMEM
    steps = ring // 2 + 1
    return pl.pallas_call(
        functools.partial(kernel, groups, span_z),
        out_shape=jax.ShapeDtypeStruct((rows, width), bf16),
        in_specs=[pl.BlockSpec(memory_space=pltpu.HBM)] * 7,
        out_specs=pl.BlockSpec(memory_space=pltpu.VMEM),
        scratch_shapes=[
            pltpu.SMEM(span_anchor.shape, jnp.int32),
            pltpu.SMEM(radial_mask.shape, jnp.int32),
            vmem((1, width), f32),
            vmem((2, rows, width), bf16),
            vmem((MEMBERS, rows, width), bf16),
            vmem((groups, 2, rows, 256), bf16),
            vmem((groups, MEMBERS, rows, 256), bf16),
            vmem((ring, 2, WIDTH, TILE), bf16),
            vmem((2 * HEAD_DIM, 2 * QUERIES), bf16),
            vmem((2 * HEAD_DIM, 2 * QUERIES), bf16),
            vmem((HEADS_HERE, HEAD_DIM, QUERIES), f32),
            vmem((MEMBERS, 2, WIDTH // 2 + 16, TILE), bf16),
            vmem((2, MEMBERS, WIDTH // 2 + 16, TILE), bf16),
            vmem((2, WIDTH, width), bf16),
            vmem((PARTS, groups // 2, rows, width // PARTS), bf16),
            vmem((PARTS, groups // 2, rows, width // PARTS), bf16),
            dma((3,)),
            dma((3,)),
            dma,
            dma,
            dma,
            dma,
            dma,
            dma((2,)),
            dma,
            dma,
            dma((2, PIECES, steps)),
            dma((2, PIECES, steps)),
            dma((MEMBERS, 2)),
            dma((MEMBERS, 2)),
            dma((2 * MEMBERS,)),
            dma((PARTS,)),
            dma((PARTS,)),
            dma((PARTS,)),
        ],
        compiler_params=pltpu.CompilerParams(
            collective_id=0, has_side_effects=True, vmem_limit_bytes=48000 * 1024
        ),
        name="radial_attention",
    )(
        *[
            pltpu.with_memory_space_constraint(x, pltpu.HBM)
            for x in (
                span_anchor,
                radial_mask,
                query_rows,
                key_rows,
                value_rows,
                out_weight,
                out_gate.reshape(1, width),
            )
        ]
    )


def solution(mesh):
    return jax.shard_map(
        body,
        mesh=mesh,
        in_specs=(
            P(("blk", "head"), None),
            P(("blk", "head"), None),
            P(("blk", "head"), None),
            P("head", None),
            P(),
            P(),
            P(),
        ),
        out_specs=P(("blk", "head"), None),
        check_vma=False,
    )
```
